256 devices in a mesh: worker: 8 (over z_lo, core), fsdp: 32 (over x, y, z_hi).
Axes of the slice: x: 4, y: 4, z: 8 (z_hi: 2, z_lo: 4; z = z_hi * 4 + z_lo), core: 2. Of those that a mesh axis runs over, the one named last changes fastest.
Arguments:
- features: bfloat16 [49152, 8192], P(('worker', 'fsdp')), may hold values from -24 to 24
- value_cotangent: bfloat16 [49152, 512], P(('worker', 'fsdp')), may hold values from -6 to 6
- value_weight: float32 [8, 8192, 512], P('worker', 'fsdp'), may hold values from -0.25 to 0.25
- first_moment: float32 [8, 8192, 512], P('worker', 'fsdp'), may hold values from -48 to 48
- second_moment: float32 [8, 8192, 512], P('worker', 'fsdp'), may hold values from 1000 to 10000
- fragment_local: float32 [8, 8192, 512], P('worker', 'fsdp'), may hold values from -6 to 6
- fragment_anchor: float32 [8192, 512], P('fsdp'), may hold values from -6 to 6
- outer_momentum: float32 [8192, 512], P('fsdp'), may hold values from -3 to 3
Outputs:
- feature_grad: float32 [49152, 8192], P(('worker', 'fsdp'))
- new_weight: float32 [8, 8192, 512], P('worker', 'fsdp')
- new_first: float32 [8, 8192, 512], P('worker', 'fsdp')
- new_second: float32 [8, 8192, 512], P('worker', 'fsdp')
- new_anchor: float32 [8192, 512], P('fsdp')
- new_momentum: float32 [8192, 512], P('fsdp')
The draws below stay inside these ranges and needn't reach their ends.
All inputs are finite; a program needn't handle non-finite values.
Results may differ from the reference program's by a relative error of at most 0.0003.
Values may be sent and summed in bfloat16 or wider, within the bound.
A program may use at most 128 MiB of HBM per device.

```python
import math
import jax
import jax.numpy as jnp
from jax import lax

D = 8192
VCOLS = 512
TOK_DEV = 192
WORKERS = 8
TOKENS = 49152
N_WORKER = 8
N_FSDP = 32


def spiked(entries, stream_key, source, target, shards_of, factor):
    owner, partner = [(jnp.arange(entries.shape[position]) // (entries.shape[position] // shards_of)).reshape([-1 if axis == position else 1 for axis in range(entries.ndim)]) for position in (source, target)]
    chosen = jax.random.permutation(stream_key, shards_of)[partner]
    strong = (owner == chosen) | (owner == (partner + shards_of // 2) % shards_of)
    return jnp.where(strong, factor * entries, entries)


def shard_levels(rng, shape, split, smallest, largest):
    def one(axis_at, shards_of):
        heights = jax.random.uniform(jax.random.fold_in(jax.random.fold_in(rng, 6), axis_at), (shards_of,), jnp.float32, smallest / len(split), largest / len(split))
        return jnp.repeat(jnp.exp(heights), shape[axis_at] // shards_of).reshape((-1,) + (1,) * (len(shape) - axis_at - 1))

    loudness = one(*split[0])
    for cut in split[1:]:
        loudness = loudness * one(*cut)
    return loudness


def scatter_about(own_key, shape, scale, most, split=(), kind=jnp.bfloat16):
    loudness = shard_levels(own_key, shape, split, -0.22, 0.18) if split else 1.0
    result = jax.random.normal(own_key, shape, jnp.float32) * scale * loudness
    return jnp.minimum(jnp.maximum(result, -most), most).astype(kind)


def gaussian_with(key, shape, deviation, reach, cuts, heavy, kind=jnp.bfloat16):
    values = deviation * jax.random.normal(key, shape, jnp.float32)
    if cuts:
        values = values * shard_levels(key, shape, cuts, -0.22, 0.18)
    return jnp.clip(spiked(values, jax.random.fold_in(key, 3), *heavy), -reach, reach).astype(kind)


def setup_inputs(seed: int = 0) -> dict:
    keys = jax.random.split(jax.random.key(seed), 9)
    features = gaussian_with(keys[0], (TOKENS, D), 1.0, 24.0, ((0, 256),), (0, 1, 256, 6.0))
    value_cotangent = scatter_about(keys[1], (TOKENS, VCOLS), 1.0, 6.0, ((0, 256),))
    value_weight = scatter_about(keys[2], (WORKERS, D, VCOLS), VCOLS ** -0.5, 0.25, ((0, 8), (1, 32)), jnp.float32)
    first_moment = scatter_about(keys[3], (WORKERS, D, VCOLS), 8.0, 48.0, ((0, 8), (1, 32)), jnp.float32)
    second_moment = jnp.clip(jnp.exp(math.log(10000.0) - 2.3025851 * jax.random.uniform(keys[4], (WORKERS, D, VCOLS), jnp.float32) ** shard_levels(keys[4], (WORKERS, D, VCOLS), ((0, 8), (1, 32)), -0.2, 0.2)), 1000.0, 10000.0)
    fragment_local = scatter_about(keys[5], (WORKERS, D, VCOLS), 1.0, 6.0, ((0, 8), (1, 32)), jnp.float32)
    fragment_anchor = scatter_about(keys[6], (D, VCOLS), 1.0, 6.0, ((0, 32),), jnp.float32)
    outer_momentum = scatter_about(keys[7], (D, VCOLS), 0.5, 3.0, ((0, 32),), jnp.float32)
    return dict(features=features, value_cotangent=value_cotangent, value_weight=value_weight, first_moment=first_moment, second_moment=second_moment, fragment_local=fragment_local, fragment_anchor=fragment_anchor, outer_momentum=outer_momentum)


first_decay = 0.9
second_decay = 0.95
inner_rate = 0.001
weight_decay = 0.1
adam_epsilon = 1e-08
adam_count = 10.0
outer_rate = 0.7
outer_mass = 0.9

def reference(features, value_cotangent, value_weight, first_moment, second_moment, fragment_local, fragment_anchor, outer_momentum):
    group_rows = TOK_DEV * N_FSDP
    grads_out = []
    weights_out = []
    firsts_out = []
    seconds_out = []
    for worker_id in range(N_WORKER):
        rows_in = features[worker_id * group_rows:(worker_id + 1) * group_rows]
        rows_cot = value_cotangent[worker_id * group_rows:(worker_id + 1) * group_rows]
        weight = value_weight[worker_id]
        grads_out.append(jnp.dot(rows_cot.astype(jnp.float32), weight.T, preferred_element_type=jnp.float32, precision=lax.Precision.HIGHEST))
        gradient = jnp.dot(rows_in.T, rows_cot, preferred_element_type=jnp.float32)
        first_new = first_decay * first_moment[worker_id] + (1.0 - first_decay) * gradient
        second_new = second_decay * second_moment[worker_id] + (1.0 - second_decay) * gradient * gradient
        first_hat = first_new / (1.0 - first_decay ** adam_count)
        second_hat = second_new / (1.0 - second_decay ** adam_count)
        weights_out.append(weight - inner_rate * (first_hat / (jnp.sqrt(second_hat) + adam_epsilon) + weight_decay * weight))
        firsts_out.append(first_new)
        seconds_out.append(second_new)
    pseudo_mean = lax.optimization_barrier(jnp.sum(fragment_anchor[None] - fragment_local, axis=0)) / N_WORKER
    new_momentum = outer_mass * outer_momentum + pseudo_mean
    new_anchor = fragment_anchor - outer_rate * (pseudo_mean + outer_mass * new_momentum)
    return (jnp.concatenate(grads_out, axis=0), jnp.stack(weights_out), jnp.stack(firsts_out), jnp.stack(seconds_out), new_anchor, new_momentum)
```

```python
import jax
import jax.numpy as jnp
from jax import lax
from jax.experimental import pallas as pl
from jax.experimental.pallas import tpu as pltpu
from jax.sharding import PartitionSpec as P

MESH = pl.DeviceIdType.MESH
F32 = jnp.float32
BF16 = jnp.bfloat16

first_decay = 0.9
second_decay = 0.95
inner_rate = 0.001
weight_decay = 0.1
adam_epsilon = 1e-08
adam_count = 10.0
outer_rate = 0.7
outer_mass = 0.9

RING = 4
TOK = 192
ROWS = 256
COLS = 512
WORKERS = 8
PART = ROWS // WORKERS

_count = 0


def _take(n):
    global _count
    base = _count
    _count += n
    return base


S_FEAT = _take(2 * 3 * RING)
S_COT1 = _take(4)
S_COT2 = _take(4)
S_WZ = _take(1)
S_W1 = _take(4)
S_W2 = _take(4)
S_R1 = _take(4)
S_R2 = _take(4)
S_GZ = _take(1)
S_OUT = _take(2 * 3 * RING)
S_LOC = _take(WORKERS - 1)
S_PSE = _take(WORKERS - 1)
N_REMOTE = _count

L_FEAT = 0
L_COT = 8
L_W = 10
L_IN = 11
L_OUT = 17
L_RES = 25
N_LOCAL = 30


def kernel(
    f_ref, c_ref, w_ref, fm_ref, sm_ref, fl_ref, fa_ref, om_ref,
    fg_ref, nw_ref, nf_ref, ns_ref, na_ref, nm_ref,
    fb, cb, wb, gb, rh, rf, zr, ob, wv, fmv, smv, fav, omv, fr, ps,
    nwv, nfv, nsv, nav, nmv,
    ssem, rsem, lsem,
):
    worker = lax.axis_index("worker")
    place = lax.axis_index("fsdp")
    x, y, zh = place // 8, (place // 2) % RING, place % 2

    zo = (zh, 1 - zh)
    gat = tuple(x * (1 - z) + y * z for z in zo)
    exc = tuple(y * (1 - z) + x * z for z in zo)

    def along_gather(o, d):
        z = zo[o]
        xx, yy = (x + d * (1 - z)) % RING, (y + d * z) % RING
        return (worker, (xx * RING + yy) * 2 + zh)

    def along_exchange(o, d):
        z = zo[o]
        xx, yy = (x + d * z) % RING, (y + d * (1 - z)) % RING
        return (worker, (xx * RING + yy) * 2 + zh)

    partner = (worker, place + 1 - 2 * zh)

    def other_worker(j):
        return ((worker + j) % WORKERS, place)

    def column(o, g, e):
        z = zo[o]
        start = g * (2048 - 1536 * z) + e * (512 + 1536 * z) + z * ROWS
        return pl.ds(pl.multiple_of(start, ROWS), ROWS)

    def tokens(e, half=None):
        if half is None:
            return pl.ds(pl.multiple_of(e * TOK, 16), TOK)
        return pl.ds(pl.multiple_of(e * TOK + half * (TOK // 2), 16), TOK // 2)

    sent = []

    def send(src, dst, sem, device):
        copy = pltpu.make_async_remote_copy(
            src_ref=src, dst_ref=dst, send_sem=ssem.at[sem], recv_sem=rsem.at[sem],
            device_id=device, device_id_type=MESH,
        )
        copy.start()
        sent.append(copy)
        return copy

    def local(src, dst, sem):
        copy = pltpu.make_async_copy(src, dst, lsem.at[sem])
        copy.start()
        return copy

    barrier = pltpu.get_barrier_semaphore()
    peers = [along_gather(0, d) for d in (1, 2, 3)] + [along_exchange(0, d) for d in (1, 2, 3)]
    peers += [partner] + [other_worker(j) for j in range(1, WORKERS)]
    for peer in peers:
        pl.semaphore_signal(barrier, inc=1, device_id=peer, device_id_type=MESH)

    cot_here = [local(c_ref, cb.at[o, tokens(exc[o])], L_COT + o) for o in range(2)]
    w_here = local(w_ref, wb.at[0, gat[0]], L_W)
    feat_here = [
        local(f_ref.at[:, column(o, g, exc[o])], fb.at[o, g, tokens(exc[o])], L_FEAT + o * RING + g)
        for o in range(2)
        for g in range(RING)
    ]
    ins = [
        local(src, dst, L_IN + i)
        for i, (src, dst) in enumerate(
            ((w_ref, wv), (fm_ref, fmv), (sm_ref, smv), (fa_ref, fav), (om_ref, omv),
             (fl_ref.at[pl.ds(pl.multiple_of(worker * PART, 8), PART)], fr.at[0]))
        )
    ]
    pl.semaphore_wait(barrier, len(peers))

    side = (1, RING - 1)
    cot1 = [
        [send(c_ref, cb.at[o, tokens(exc[o])], S_COT1 + 2 * o + i, along_exchange(o, side[i])) for i in range(2)]
        for o in range(2)
    ]
    wz = send(w_ref, wb.at[1, gat[0]], S_WZ, partner)
    loc = [
        send(
            fl_ref.at[pl.ds(pl.multiple_of((worker + j) % WORKERS * PART, 8), PART)],
            fr.at[j], S_LOC + j - 1, other_worker(j),
        )
        for j in range(1, WORKERS)
    ]
    feat = []
    for d in (2, 1, 3):
        for o in range(2):
            for g in range(RING):
                feat.append(
                    send(
                        f_ref.at[:, column(o, g, (exc[o] + d) % RING)],
                        fb.at[o, g, tokens(exc[o])],
                        S_FEAT + (o * 3 + d - 1) * RING + g,
                        along_exchange(o, d),
                    )
                )
    w1 = [[send(w_ref, wb.at[0, gat[0]], S_W1 + i, along_gather(0, side[i])) for i in range(2)], None]

    for copy in cot_here:
        copy.wait()
    cot2 = []
    for o in range(2):
        for i in range(2):
            cot1[o][i].wait_recv()
            block = (exc[o] + RING - side[i]) % RING
            rows = cb.at[o, tokens(block, i)]
            cot2.append(send(rows, rows, S_COT2 + 2 * o + i, along_exchange(o, side[i])))

    for copy in ins:
        copy.wait()
    total = jnp.zeros((PART, COLS), F32)
    anchor = fav[pl.ds(pl.multiple_of(worker * PART, 8), PART), :]
    for j in range(WORKERS):
        if j:
            loc[j - 1].wait_recv()
        total = total + (anchor - fr[j])
    mine = pl.ds(pl.multiple_of(worker * PART, 8), PART)
    ps[mine, :] = total
    pse = [send(ps.at[mine], ps.at[mine], S_PSE + j - 1, other_worker(j)) for j in range(1, WORKERS)]

    for copy in feat_here:
        copy.wait()
    for copy in feat + cot2:
        copy.wait_recv()

    def partial(o, g):
        gb[o, g] = lax.dot_general(
            fb[o, g], cb[o], (((0,), (0,)), ((), ())), preferred_element_type=F32
        )

    half = ROWS // 2
    r1 = [[], []]
    for o in range(2):
        far = (gat[o] + 2) % RING
        partial(o, far)
        for i in range(2):
            r1[o].append(
                send(gb.at[o, far, pl.ds(i * half, half)], rh.at[o, i], S_R1 + 2 * o + i, along_gather(o, side[i]))
            )

    wz.wait_recv()
    w1[1] = [
        send(wb.at[1, gat[1]], wb.at[1, gat[1]], S_W1 + 2 + i, along_gather(1, side[i])) for i in range(2)
    ]

    for o in range(2):
        for i in range(2):
            partial(o, (gat[o] + side[i]) % RING)
    w_here.wait()
    w2 = [[], []]
    r2 = [[], []]

    def forward_w(o):
        for i in range(2):
            w1[o][i].wait_recv()
            block = (gat[o] + RING - side[i]) % RING
            rows = wb.at[o, block, pl.ds(i * half, half)]
            w2[o].append(send(rows, rows, S_W2 + 2 * o + i, along_gather(o, side[i])))

    def pass_on(o):
        for i in range(2):
            r1[o][i].wait_recv()
            block = (gat[o] + side[i]) % RING
            gb[o, block, pl.ds(i * half, half), :] = gb[o, block, pl.ds(i * half, half), :] + rh[o, i]
            r2[o].append(send(gb.at[o, block], rf.at[o, i], S_R2 + 2 * o + i, along_gather(o, side[i])))

    forward_w(0)
    pass_on(0)
    pass_on(1)
    for o in range(2):
        partial(o, gat[o])
    forward_w(1)

    out = []
    out_here = []

    def product(o):
        for g in range(RING):
            w = wb[o, g]
            high = w.astype(BF16)
            low = (w - high.astype(F32)).astype(BF16)
            dims = (((1,), (1,)), ((), ()))
            c = cb[o]
            ob[o, g] = lax.dot_general(c, high, dims, preferred_element_type=F32) + lax.dot_general(
                c, low, dims, preferred_element_type=F32
            )
            there = fg_ref.at[:, column(o, g, exc[o])]
            for d in (2, 1, 3):
                out.append(
                    send(
                        ob.at[o, g, tokens((exc[o] + d) % RING)], there,
                        S_OUT + (o * 3 + d - 1) * RING + g, along_exchange(o, d),
                    )
                )
            out_here.append(local(ob.at[o, g, tokens(exc[o])], there, L_OUT + o * RING + g))

    for copy in w2[0]:
        copy.wait_recv()
    product(0)

    for copy in r2[1]:
        copy.wait_recv()
    gb[1, gat[1]] = gb[1, gat[1]] + rf[1, 0] + rf[1, 1]
    gz = send(gb.at[1, gat[1]], zr, S_GZ, partner)

    for copy in w2[1]:
        copy.wait_recv()
    product(1)

    for copy in pse:
        copy.wait_recv()
    pseudo = ps[...] / WORKERS
    momentum = outer_mass * omv[...] + pseudo
    nmv[...] = momentum
    nav[...] = fav[...] - outer_rate * (pseudo + outer_mass * momentum)
    results = [local(nmv, nm_ref, L_RES), local(nav, na_ref, L_RES + 1)]

    for copy in r2[0]:
        copy.wait_recv()
    plane = gb[0, gat[0]] + rf[0, 0] + rf[0, 1]
    gz.wait_recv()
    gradient = plane + zr[...]
    weight = wv[...]
    first_new = first_decay * fmv[...] + (1.0 - first_decay) * gradient
    second_new = second_decay * smv[...] + (1.0 - second_decay) * gradient * gradient
    first_hat = first_new / (1.0 - first_decay**adam_count)
    second_hat = second_new / (1.0 - second_decay**adam_count)
    nfv[...] = first_new
    nsv[...] = second_new
    nwv[...] = weight - inner_rate * (first_hat / (jnp.sqrt(second_hat) + adam_epsilon) + weight_decay * weight)
    results += [local(nfv, nf_ref, L_RES + 2), local(nsv, ns_ref, L_RES + 3), local(nwv, nw_ref, L_RES + 4)]

    for copy in out:
        copy.wait_recv()
    for copy in results + out_here:
        copy.wait()
    for copy in sent:
        copy.wait_send()


def on_device(
    features, value_cotangent, value_weight, first_moment, second_moment, fragment_local, fragment_anchor,
    outer_momentum,
):
    hbm = pl.BlockSpec(memory_space=pltpu.HBM)
    param = jax.ShapeDtypeStruct((ROWS, COLS), F32)
    vparam = pltpu.VMEM((ROWS, COLS), F32)
    got = pl.pallas_call(
        kernel,
        name="backward",
        out_shape=(jax.ShapeDtypeStruct(features.shape, F32),) + (param,) * 5,
        in_specs=[hbm] * 8,
        out_specs=(hbm,) * 6,
        scratch_shapes=[
            pltpu.VMEM((2, RING, RING * TOK, ROWS), BF16),
            pltpu.VMEM((2, RING * TOK, COLS), BF16),
            pltpu.VMEM((2, RING, ROWS, COLS), F32),
            pltpu.VMEM((2, RING, ROWS, COLS), F32),
            pltpu.VMEM((2, 2, ROWS // 2, COLS), F32),
            pltpu.VMEM((2, 2, ROWS, COLS), F32),
            vparam,
            pltpu.VMEM((2, RING, RING * TOK, ROWS), F32),
            vparam, vparam, vparam, vparam, vparam,
            pltpu.VMEM((WORKERS, PART, COLS), F32),
            vparam,
            vparam, vparam, vparam, vparam, vparam,
            pltpu.SemaphoreType.DMA((N_REMOTE,)),
            pltpu.SemaphoreType.DMA((N_REMOTE,)),
            pltpu.SemaphoreType.DMA((N_LOCAL,)),
        ],
        compiler_params=pltpu.CompilerParams(
            collective_id=0, has_side_effects=True, vmem_limit_bytes=56 * 2**20
        ),
    )(
        features, value_cotangent, value_weight[0], first_moment[0], second_moment[0], fragment_local[0],
        fragment_anchor, outer_momentum,
    )
    feature_grad, weight_new, first_new, second_new, new_anchor, new_momentum = got
    return feature_grad, weight_new[None], first_new[None], second_new[None], new_anchor, new_momentum


def solution(mesh):
    tokens = P(("worker", "fsdp"), None)
    groups = P("worker", "fsdp", None)
    whole = P("fsdp", None)
    return jax.shard_map(
        on_device,
        mesh=mesh,
        in_specs=(tokens, tokens, groups, groups, groups, groups, whole, whole),
        out_specs=(tokens, groups, groups, groups, whole, whole),
        check_vma=False,
    )
```

```python
import jax
import jax.numpy as jnp
from jax import lax
from jax.experimental import pallas as pl
from jax.experimental.pallas import tpu as pltpu
from jax.sharding import PartitionSpec as P

MESH = pl.DeviceIdType.MESH
F32 = jnp.float32
BF16 = jnp.bfloat16

first_decay = 0.9
second_decay = 0.95
inner_rate = 0.001
weight_decay = 0.1
adam_epsilon = 1e-08
adam_count = 10.0
outer_rate = 0.7
outer_mass = 0.9

RING = 4
TOK = 192
ROWS = 256
COLS = 512
WORKERS = 8
PART = ROWS // WORKERS

_count = 0


def _take(n):
    global _count
    base = _count
    _count += n
    return base


S_FEAT = _take(2 * 3 * RING)
S_COT1 = _take(8)
S_COT2 = _take(4)
S_WZ = _take(2)
S_W1 = _take(8)
S_W2 = _take(4)
S_R1 = _take(4)
S_R2 = _take(8)
S_GZ = _take(1)
S_OUT = _take(2 * 3 * RING)
S_LOC = _take(WORKERS - 1)
S_PSE = _take(WORKERS - 1)
N_REMOTE = _count

L_FEAT = 0
L_COT = 8
L_W = 10
L_IN = 11
L_OUT = 17
L_RES = 25
N_LOCAL = 30

STEPS = 30847.0
MARK = 16


def encode(t):
    largest = jnp.max(jnp.abs(t), axis=0, keepdims=True)
    unit = jnp.maximum(largest * 1.01, 1e-30).astype(BF16).astype(F32)
    q = t * (STEPS / unit)
    n = jnp.minimum(jnp.floor(jnp.abs(q) + 0.5), STEPS)
    e = jnp.floor(n * (1.0 / 128.0))
    size = (1.0 + (n - 128.0 * e) * (1.0 / 128.0)) * jnp.exp2(e - 120.0)
    return jnp.where(q < 0, -size, size).astype(BF16), unit


def store_code(ref, t):
    code, unit = encode(t)
    rows = t.shape[0]
    ref[pl.ds(0, rows), :] = code
    ref[pl.ds(rows, MARK), :] = jnp.broadcast_to(unit, (MARK, t.shape[1])).astype(BF16)


def load_code(ref):
    rows = ref.shape[0] - MARK
    unit = ref[pl.ds(rows, MARK), :].astype(F32)[0:1]
    return decode(ref[pl.ds(0, rows), :], unit)


def decode(code, unit):
    v = code.astype(F32)
    a = jnp.abs(v)
    e = jnp.floor(jnp.log(a) * 1.4426950408889634 + 0.0025)
    n = jnp.floor(a * jnp.exp2(7.0 - e) + 0.5) + (e * 128.0 + 119.0 * 128.0)
    n = n * (unit * (1.0 / STEPS))
    return jnp.where(v < 0, -n, n)


def kernel(
    f_ref, c_ref, w_ref, fm_ref, sm_ref, fl_ref, fa_ref, om_ref,
    code_ref, nw_ref, nf_ref, ns_ref, na_ref, nm_ref,
    fb, cb, wb, gb, rh, rf, zr, ob, high, low, wv, fmv, smv, fav, omv, fr, ps,
    nwv, nfv, nsv, nav, nmv,
    ssem, rsem, lsem,
):
    worker = lax.axis_index("worker")
    place = lax.axis_index("fsdp")
    x, y, zh = place // 8, (place // 2) % RING, place % 2

    zo = (zh, 1 - zh)
    gat = tuple(x * (1 - z) + y * z for z in zo)
    exc = tuple(y * (1 - z) + x * z for z in zo)

    def along_gather(o, d):
        z = zo[o]
        xx, yy = (x + d * (1 - z)) % RING, (y + d * z) % RING
        return (worker, (xx * RING + yy) * 2 + zh)

    def along_exchange(o, d):
        z = zo[o]
        xx, yy = (x + d * z) % RING, (y + d * (1 - z)) % RING
        return (worker, (xx * RING + yy) * 2 + zh)

    partner = (worker, place + 1 - 2 * zh)

    def other_worker(j):
        return ((worker + j) % WORKERS, place)

    def column(o, g, e):
        z = zo[o]
        start = g * (2048 - 1536 * z) + e * (512 + 1536 * z) + z * ROWS
        return pl.ds(pl.multiple_of(start, ROWS), ROWS)

    def slab(o, g, e):
        z = zo[o]
        return g * (8 - 6 * z) + e * (2 + 6 * z) + z

    def tokens(e, half=None):
        if half is None:
            return pl.ds(pl.multiple_of(e * TOK, 16), TOK)
        return pl.ds(pl.multiple_of(e * TOK + half * (TOK // 2), 16), TOK // 2)

    sent = []

    def send(src, dst, sem, device):
        copy = pltpu.make_async_remote_copy(
            src_ref=src, dst_ref=dst, send_sem=ssem.at[sem], recv_sem=rsem.at[sem],
            device_id=device, device_id_type=MESH,
        )
        copy.start()
        sent.append(copy)
        return copy

    def local(src, dst, sem):
        copy = pltpu.make_async_copy(src, dst, lsem.at[sem])
        copy.start()
        return copy

    barrier = pltpu.get_barrier_semaphore()
    peers = [along_gather(0, d) for d in (1, 2, 3)] + [along_exchange(0, d) for d in (1, 2, 3)]
    peers += [partner] + [other_worker(j) for j in range(1, WORKERS)]
    for peer in peers:
        pl.semaphore_signal(barrier, inc=1, device_id=peer, device_id_type=MESH)

    cot_here = [local(c_ref, cb.at[o, tokens(exc[o])], L_COT + o) for o in range(2)]
    w_here = local(w_ref, wv, L_W)
    feat_here = [
        local(f_ref.at[:, column(o, g, exc[o])], fb.at[o, g, tokens(exc[o])], L_FEAT + o * RING + g)
        for o in range(2)
        for g in range(RING)
    ]
    ins = [
        local(src, dst, L_IN + i)
        for i, (src, dst) in enumerate(
            ((fm_ref, fmv), (sm_ref, smv), (fa_ref, fav), (om_ref, omv),
             (fl_ref.at[pl.ds(pl.multiple_of(worker * PART, 8), PART)], fr.at[0]))
        )
    ]
    pl.semaphore_wait(barrier, len(peers))

    side = (1, RING - 1)
    half = ROWS // 2

    def halves(i):
        return (i, 1 - i)

    cot1 = {}
    for part in range(2):
        for o in range(2):
            for i in range(2):
                h = halves(i)[part]
                cot1[o, i, h] = send(
                    c_ref.at[pl.ds(h * (TOK // 2), TOK // 2)], cb.at[o, tokens(exc[o], h)],
                    S_COT1 + 4 * o + 2 * i + h, along_exchange(o, side[i]),
                )
    w_here.wait()
    for h in range(2):
        store_code(wb.at[0, gat[0], h], wv[pl.ds(h * half, half), :])
    wz = [send(wb.at[0, gat[0], h], wb.at[1, gat[0], h], S_WZ + h, partner) for h in range(2)]
    feat = []
    for d in (2, 1, 3):
        for o in range(2):
            for g in range(RING):
                feat.append(
                    send(
                        f_ref.at[:, column(o, g, (exc[o] + d) % RING)],
                        fb.at[o, g, tokens(exc[o])],
                        S_FEAT + (o * 3 + d - 1) * RING + g,
                        along_exchange(o, d),
                    )
                )

    for copy in cot_here:
        copy.wait()
    cot2 = []
    for o in range(2):
        for i in range(2):
            cot1[o, i, i].wait_recv()
            rows = cb.at[o, tokens((exc[o] + RING - side[i]) % RING, i)]
            cot2.append(send(rows, rows, S_COT2 + 2 * o + i, along_exchange(o, side[i])))
    loc = [
        send(
            fl_ref.at[pl.ds(pl.multiple_of((worker + j) % WORKERS * PART, 8), PART)],
            fr.at[j], S_LOC + j - 1, other_worker(j),
        )
        for j in range(1, WORKERS)
    ]

    def multiply(o, g):
        for h in range(2):
            w = load_code(wb.at[o, g, h])
            top = w.astype(BF16)
            high[pl.ds(h * half, half), :] = top
            low[pl.ds(h * half, half), :] = (w - top.astype(F32)).astype(BF16)
        dims = (((1,), (1,)), ((), ()))

        def step(e, carry):
            c = cb[o, tokens(e)]
            t = lax.dot_general(c, high[...], dims, preferred_element_type=F32) + lax.dot_general(
                c, low[...], dims, preferred_element_type=F32
            )
            store_code(ob.at[o, g, e], t)
            return carry

        lax.fori_loop(0, RING, step, 0)

    out = []
    out_here = []

    def give(o, g, at):
        there = code_ref.at[slab(o, g, exc[o])]
        for d in (2, 1, 3):
            out.append(
                send(
                    ob.at[o, g, (exc[o] + d) % RING], there,
                    S_OUT + (o * 3 + d - 1) * RING + at, along_exchange(o, d),
                )
            )
        out_here.append(local(ob.at[o, g, exc[o]], there, L_OUT + o * RING + at))

    def product(o, at):
        g = (gat[o] + at) % RING
        multiply(o, g)
        give(o, g, at)

    for copy in feat_here:
        copy.wait()
    for key in cot1:
        if key[1] != key[2]:
            cot1[key].wait_recv()
    for copy in cot2:
        copy.wait_recv()
    multiply(0, gat[0])
    for copy in feat:
        copy.wait_recv()

    def partial(o, g):
        gb[o, g] = lax.dot_general(
            fb[o, g], cb[o], (((0,), (0,)), ((), ())), preferred_element_type=F32
        )

    r1, r2 = {}, {}
    for o in range(2):
        far = (gat[o] + 2) % RING
        partial(o, far)
        for i in range(2):
            r1[o, i] = send(
                gb.at[o, far, pl.ds(i * half, half)], rh.at[o, i], S_R1 + 2 * o + i, along_gather(o, side[i])
            )

    def hand(o, i, h):
        block = (gat[o] + side[i]) % RING
        r2[o, i, h] = send(
            gb.at[o, block, pl.ds(h * half, half)], rf.at[o, i, pl.ds(h * half, half)],
            S_R2 + 4 * o + 2 * i + h, along_gather(o, side[i]),
        )

    for o in range(2):
        for i in range(2):
            partial(o, (gat[o] + side[i]) % RING)
            hand(o, i, 1 - i)
    for o in range(2):
        for i in range(2):
            r1[o, i].wait_recv()
            block = (gat[o] + side[i]) % RING
            rows = pl.ds(i * half, half)
            gb[o, block, rows, :] = gb[o, block, rows, :] + rh[o, i]
            hand(o, i, i)

    w1, w2 = {}, {}

    def weights(o):
        for part in range(2):
            for i in range(2):
                h = halves(i)[part]
                rows = wb.at[o, gat[o], h]
                w1[o, i, h] = send(rows, rows, S_W1 + 4 * o + 2 * i + h, along_gather(o, side[i]))

    def forward(o):
        for i in range(2):
            w1[o, i, i].wait_recv()
            rows = wb.at[o, (gat[o] + RING - side[i]) % RING, i]
            w2[o, i] = send(rows, rows, S_W2 + 2 * o + i, along_gather(o, side[i]))

    weights(0)
    for copy in wz:
        copy.wait_recv()
    weights(1)
    give(0, gat[0], 0)
    for o in range(2):
        partial(o, gat[o])

    for copy in ins:
        copy.wait()
    mine = pl.ds(pl.multiple_of(worker * PART, 8), PART)
    anchor = fav[mine, :]
    total = anchor - fr[0]
    for j in range(1, WORKERS):
        loc[j - 1].wait_recv()
        total = total + (anchor - fr[j])
    ps[mine, :] = total

    def plane(o):
        for i in range(2):
            for h in range(2):
                r2[o, i, h].wait_recv()
        return gb[o, gat[o]] + rf[o, 0] + rf[o, 1]

    forward(0)
    gb[1, gat[1]] = plane(1)
    gz = send(gb.at[1, gat[1]], zr, S_GZ, partner)
    forward(1)
    pse = [send(ps.at[mine], ps.at[mine], S_PSE + j - 1, other_worker(j)) for j in range(1, WORKERS)]

    product(1, 0)
    for i in range(2):
        for o in range(2):
            w1[o, 1 - i, i].wait_recv()
            product(o, side[i])
    gb[0, gat[0]] = plane(0)
    for o in range(2):
        for i in range(2):
            w2[o, i].wait_recv()
        product(o, 2)

    for copy in pse:
        copy.wait_recv()
    pseudo = ps[...] / WORKERS
    momentum = outer_mass * omv[...] + pseudo
    nmv[...] = momentum
    nav[...] = fav[...] - outer_rate * (pseudo + outer_mass * momentum)
    results = [local(nmv, nm_ref, L_RES), local(nav, na_ref, L_RES + 1)]

    gz.wait_recv()
    gradient = gb[0, gat[0]] + zr[...]
    weight = wv[...]
    first_new = first_decay * fmv[...] + (1.0 - first_decay) * gradient
    second_new = second_decay * smv[...] + (1.0 - second_decay) * gradient * gradient
    first_hat = first_new / (1.0 - first_decay**adam_count)
    second_hat = second_new / (1.0 - second_decay**adam_count)
    nfv[...] = first_new
    nsv[...] = second_new
    nwv[...] = weight - inner_rate * (first_hat / (jnp.sqrt(second_hat) + adam_epsilon) + weight_decay * weight)
    results += [local(nfv, nf_ref, L_RES + 2), local(nsv, ns_ref, L_RES + 3), local(nwv, nw_ref, L_RES + 4)]

    for copy in out:
        copy.wait_recv()
    for copy in results + out_here:
        copy.wait()
    for copy in sent:
        copy.wait_send()


GROUP = 4


def finish(code_ref, *refs):
    fg_ref = refs[5]
    code, wide, stage, sems = refs[11:]
    groups = code_ref.shape[0] // GROUP
    loads = [
        pltpu.make_async_copy(code_ref.at[pl.ds(i * GROUP, GROUP)], code.at[pl.ds(i * GROUP, GROUP)], sems.at[0, i])
        for i in range(groups)
    ]
    stores = [
        pltpu.make_async_copy(
            wide.at[:, pl.ds(i * GROUP * ROWS, GROUP * ROWS)],
            fg_ref.at[:, pl.ds(i * GROUP * ROWS, GROUP * ROWS)],
            sems.at[1, i],
        )
        for i in range(groups)
    ]
    into = [pltpu.make_async_copy(refs[k], stage.at[k], sems.at[0, groups + k]) for k in range(5)]
    outof = [pltpu.make_async_copy(stage.at[k], refs[6 + k], sems.at[1, groups + k]) for k in range(5)]
    for copy in loads + into:
        copy.start()
    for i in range(groups):
        loads[i].wait()
        for k in range(i * GROUP, (i + 1) * GROUP):
            wide[:, pl.ds(k * ROWS, ROWS)] = load_code(code.at[k])
        stores[i].start()
        if i == groups - 2:
            for load, store in zip(into, outof):
                load.wait()
                store.start()
    for copy in stores + outof:
        copy.wait()


def on_device(
    features, value_cotangent, value_weight, first_moment, second_moment, fragment_local, fragment_anchor,
    outer_momentum,
):
    hbm = pl.BlockSpec(memory_space=pltpu.HBM)
    slabs = features.shape[1] // ROWS
    param = jax.ShapeDtypeStruct((ROWS, COLS), F32)
    vparam = pltpu.VMEM((ROWS, COLS), F32)
    got = pl.pallas_call(
        kernel,
        name="backward",
        out_shape=(jax.ShapeDtypeStruct((slabs, TOK + MARK, ROWS), BF16),) + (param,) * 5,
        in_specs=[hbm] * 8,
        out_specs=(hbm,) * 6,
        scratch_shapes=[
            pltpu.VMEM((2, RING, RING * TOK, ROWS), BF16),
            pltpu.VMEM((2, RING * TOK, COLS), BF16),
            pltpu.VMEM((2, RING, 2, ROWS // 2 + MARK, COLS), BF16),
            pltpu.VMEM((2, RING, ROWS, COLS), F32),
            pltpu.VMEM((2, 2, ROWS // 2, COLS), F32),
            pltpu.VMEM((2, 2, ROWS, COLS), F32),
            vparam,
            pltpu.VMEM((2, RING, RING, TOK + MARK, ROWS), BF16),
            pltpu.VMEM((ROWS, COLS), BF16),
            pltpu.VMEM((ROWS, COLS), BF16),
            vparam, vparam, vparam, vparam, vparam,
            pltpu.VMEM((WORKERS, PART, COLS), F32),
            vparam,
            vparam, vparam, vparam, vparam, vparam,
            pltpu.SemaphoreType.DMA((N_REMOTE,)),
            pltpu.SemaphoreType.DMA((N_REMOTE,)),
            pltpu.SemaphoreType.DMA((N_LOCAL,)),
        ],
        compiler_params=pltpu.CompilerParams(
            collective_id=0, has_side_effects=True, vmem_limit_bytes=56 * 2**20
        ),
    )(
        features, value_cotangent, value_weight[0], first_moment[0], second_moment[0], fragment_local[0],
        fragment_anchor, outer_momentum,
    )
    feature_grad, weight_new, first_new, second_new, new_anchor, new_momentum = pl.pallas_call(
        finish,
        name="finish",
        out_shape=(jax.ShapeDtypeStruct(features.shape, F32),) + (param,) * 5,
        in_specs=[hbm] * 6,
        out_specs=(hbm,) * 6,
        scratch_shapes=[
            pltpu.VMEM((slabs, TOK + MARK, ROWS), BF16),
            pltpu.VMEM(features.shape, F32),
            pltpu.VMEM((5, ROWS, COLS), F32),
            pltpu.SemaphoreType.DMA((2, slabs // GROUP + 5)),
        ],
        compiler_params=pltpu.CompilerParams(vmem_limit_bytes=60 * 2**20),
    )(*got)
    return feature_grad, weight_new[None], first_new[None], second_new[None], new_anchor, new_momentum


def solution(mesh):
    tokens = P(("worker", "fsdp"), None)
    groups = P("worker", "fsdp", None)
    whole = P("fsdp", None)
    return jax.shard_map(
        on_device,
        mesh=mesh,
        in_specs=(tokens, tokens, groups, groups, groups, groups, whole, whole),
        out_specs=(tokens, groups, groups, groups, whole, whole),
        check_vma=False,
    )
```

```python
import jax
import jax.numpy as jnp
from jax import lax
from jax.experimental import pallas as pl
from jax.experimental.pallas import tpu as pltpu
from jax.sharding import PartitionSpec as P

MESH = pl.DeviceIdType.MESH
F32 = jnp.float32
BF16 = jnp.bfloat16

first_decay = 0.9
second_decay = 0.95
inner_rate = 0.001
weight_decay = 0.1
adam_epsilon = 1e-08
adam_count = 10.0
outer_rate = 0.7
outer_mass = 0.9

RING = 4
TOK = 192
ROWS = 256
COLS = 512
WORKERS = 8
PART = ROWS // WORKERS

_count = 0


def _take(n):
    global _count
    base = _count
    _count += n
    return base


S_FEAT = _take(2 * 3 * RING)
S_COT1 = _take(8)
S_COT2 = _take(4)
S_WZ = _take(2)
S_W1 = _take(8)
S_W2 = _take(4)
S_R1 = _take(4)
S_R2 = _take(8)
S_GZ = _take(2)
S_OUT = _take(2 * 3 * RING)
S_LOC = _take(WORKERS - 1)
S_PSE = _take(WORKERS - 1)
N_REMOTE = _count

L_FEAT = 0
L_COT = 8
L_W = 10
L_IN = 11
L_OUT = 17
L_RES = 25
N_LOCAL = 30

STEPS = 30847.0
MARK = 16


def encode(t):
    largest = jnp.max(jnp.abs(t), axis=0, keepdims=True)
    unit = jnp.maximum(largest * 1.01, 1e-30).astype(BF16).astype(F32)
    q = t * (STEPS / unit)
    n = jnp.minimum(jnp.floor(jnp.abs(q) + 0.5), STEPS)
    e = jnp.floor(n * (1.0 / 128.0))
    size = (1.0 + (n - 128.0 * e) * (1.0 / 128.0)) * jnp.exp2(e - 120.0)
    return jnp.where(q < 0, -size, size).astype(BF16), unit


def store_code(ref, t):
    code, unit = encode(t)
    rows = t.shape[0]
    ref[pl.ds(0, rows), :] = code
    ref[pl.ds(rows, MARK), :] = jnp.broadcast_to(unit, (MARK, t.shape[1])).astype(BF16)


def code_of(ref, t):
    store_code(ref, t)
    return ref


def load_code(ref):
    rows = ref.shape[0] - MARK
    unit = ref[pl.ds(rows, MARK), :].astype(F32)[0:1]
    return decode(ref[pl.ds(0, rows), :], unit)


def decode(code, unit):
    v = code.astype(F32)
    a = jnp.abs(v)
    e = jnp.floor(jnp.log(a) * 1.4426950408889634 + 0.0025)
    n = jnp.floor(a * jnp.exp2(7.0 - e) + 0.5) + (e * 128.0 + 119.0 * 128.0)
    n = n * (unit * (1.0 / STEPS))
    return jnp.where(v < 0, -n, n)


def kernel(
    f_ref, c_ref, w_ref, fm_ref, sm_ref, fl_ref, fa_ref, om_ref,
    code_ref, nw_ref, nf_ref, ns_ref, na_ref, nm_ref,
    fb, cb, wb, gb, r1s, rh, r2s, rf, gs, zr, ob, high, low, wv, fmv, smv, fav, omv, fr, ps,
    nwv, nfv, nsv, nav, nmv,
    ssem, rsem, lsem,
):
    worker = lax.axis_index("worker")
    place = lax.axis_index("fsdp")
    x, y, zh = place // 8, (place // 2) % RING, place % 2

    zo = (zh, 1 - zh)
    gat = tuple(x * (1 - z) + y * z for z in zo)
    exc = tuple(y * (1 - z) + x * z for z in zo)

    def along_gather(o, d):
        z = zo[o]
        xx, yy = (x + d * (1 - z)) % RING, (y + d * z) % RING
        return (worker, (xx * RING + yy) * 2 + zh)

    def along_exchange(o, d):
        z = zo[o]
        xx, yy = (x + d * z) % RING, (y + d * (1 - z)) % RING
        return (worker, (xx * RING + yy) * 2 + zh)

    partner = (worker, place + 1 - 2 * zh)

    def other_worker(j):
        return ((worker + j) % WORKERS, place)

    def column(o, g, e):
        z = zo[o]
        start = g * (2048 - 1536 * z) + e * (512 + 1536 * z) + z * ROWS
        return pl.ds(pl.multiple_of(start, ROWS), ROWS)

    def slab(o, g, e):
        z = zo[o]
        return g * (8 - 6 * z) + e * (2 + 6 * z) + z

    def tokens(e, half=None):
        if half is None:
            return pl.ds(pl.multiple_of(e * TOK, 16), TOK)
        return pl.ds(pl.multiple_of(e * TOK + half * (TOK // 2), 16), TOK // 2)

    sent = []

    def send(src, dst, sem, device):
        copy = pltpu.make_async_remote_copy(
            src_ref=src, dst_ref=dst, send_sem=ssem.at[sem], recv_sem=rsem.at[sem],
            device_id=device, device_id_type=MESH,
        )
        copy.start()
        sent.append(copy)
        return copy

    def local(src, dst, sem):
        copy = pltpu.make_async_copy(src, dst, lsem.at[sem])
        copy.start()
        return copy

    barrier = pltpu.get_barrier_semaphore()
    peers = [along_gather(0, d) for d in (1, 2, 3)] + [along_exchange(0, d) for d in (1, 2, 3)]
    peers += [partner] + [other_worker(j) for j in range(1, WORKERS)]
    for peer in peers:
        pl.semaphore_signal(barrier, inc=1, device_id=peer, device_id_type=MESH)

    w_here = local(w_ref, wv, L_W)
    cot_here = [local(c_ref, cb.at[o, tokens(exc[o])], L_COT + o) for o in range(2)]
    feat_here = [
        local(f_ref.at[:, column(o, g, exc[o])], fb.at[o, g, tokens(exc[o])], L_FEAT + o * RING + g)
        for o in range(2)
        for g in range(RING)
    ]
    ins = [
        local(src, dst, L_IN + i)
        for i, (src, dst) in enumerate(
            ((fm_ref, fmv), (sm_ref, smv), (fa_ref, fav), (om_ref, omv),
             (fl_ref.at[pl.ds(pl.multiple_of(worker * PART, 8), PART)], fr.at[0]))
        )
    ]
    half = ROWS // 2
    w_here.wait()
    for h in range(2):
        store_code(wb.at[0, gat[0], h], wv[pl.ds(h * half, half), :])
    pl.semaphore_wait(barrier, len(peers))

    side = (1, RING - 1)

    def halves(i):
        return (i, 1 - i)

    cot1 = {}
    for part in range(2):
        for o in range(2):
            for i in range(2):
                h = halves(i)[part]
                cot1[o, i, h] = send(
                    c_ref.at[pl.ds(h * (TOK // 2), TOK // 2)], cb.at[o, tokens(exc[o], h)],
                    S_COT1 + 4 * o + 2 * i + h, along_exchange(o, side[i]),
                )
    wz = [send(wb.at[0, gat[0], h], wb.at[1, gat[0], h], S_WZ + h, partner) for h in range(2)]
    feat = {}
    for at in (2, 1, 3, 0):
        for d in (2, 1, 3):
            for o in range(2):
                feat[o, at, d] = send(
                    f_ref.at[:, column(o, (gat[o] + at) % RING, (exc[o] + d) % RING)],
                    fb.at[o, (gat[o] + at) % RING, tokens(exc[o])],
                    S_FEAT + (o * 3 + d - 1) * RING + at,
                    along_exchange(o, d),
                )

    for copy in cot_here:
        copy.wait()
    cot2 = []
    for o in range(2):
        for i in range(2):
            cot1[o, i, i].wait_recv()
            rows = cb.at[o, tokens((exc[o] + RING - side[i]) % RING, i)]
            cot2.append(send(rows, rows, S_COT2 + 2 * o + i, along_exchange(o, side[i])))
    loc = [
        send(
            fl_ref.at[pl.ds(pl.multiple_of((worker + j) % WORKERS * PART, 8), PART)],
            fr.at[j], S_LOC + j - 1, other_worker(j),
        )
        for j in range(1, WORKERS)
    ]

    def multiply(o, g):
        for h in range(2):
            w = load_code(wb.at[o, g, h])
            top = w.astype(BF16)
            high[pl.ds(h * half, half), :] = top
            low[pl.ds(h * half, half), :] = (w - top.astype(F32)).astype(BF16)
        dims = (((1,), (1,)), ((), ()))

        def step(e, carry):
            c = cb[o, tokens(e)]
            t = lax.dot_general(c, high[...], dims, preferred_element_type=F32) + lax.dot_general(
                c, low[...], dims, preferred_element_type=F32
            )
            store_code(ob.at[o, g, e], t)
            return carry

        lax.fori_loop(0, RING, step, 0)

    out = []
    out_here = []

    def give(o, g, at):
        there = code_ref.at[slab(o, g, exc[o])]
        for d in (2, 1, 3):
            out.append(
                send(
                    ob.at[o, g, (exc[o] + d) % RING], there,
                    S_OUT + (o * 3 + d - 1) * RING + at, along_exchange(o, d),
                )
            )
        out_here.append(local(ob.at[o, g, exc[o]], there, L_OUT + o * RING + at))

    def product(o, at):
        g = (gat[o] + at) % RING
        multiply(o, g)
        give(o, g, at)

    for copy in feat_here:
        copy.wait()
    for key in cot1:
        if key[1] != key[2]:
            cot1[key].wait_recv()
    for copy in cot2:
        copy.wait_recv()
    multiply(0, gat[0])

    def partial(o, at):
        g = (gat[o] + at) % RING
        for d in (2, 1, 3):
            feat[o, at, d].wait_recv()
        gb[o, g] = lax.dot_general(
            fb[o, g], cb[o], (((0,), (0,)), ((), ())), preferred_element_type=F32
        )

    r1, r2 = {}, {}
    for o in range(2):
        far = (gat[o] + 2) % RING
        partial(o, 2)
        for i in range(2):
            r1[o, i] = send(
                code_of(r1s.at[o, i], gb[o, far, pl.ds(i * half, half), :]), rh.at[o, i],
                S_R1 + 2 * o + i, along_gather(o, side[i]),
            )

    def hand(o, i, h):
        block = (gat[o] + side[i]) % RING
        r2[o, i, h] = send(
            code_of(r2s.at[o, i, h], gb[o, block, pl.ds(h * half, half), :]), rf.at[o, i, h],
            S_R2 + 4 * o + 2 * i + h, along_gather(o, side[i]),
        )

    for i in range(2):
        for o in range(2):
            partial(o, side[i])
            hand(o, i, 1 - i)
    for o in range(2):
        for i in range(2):
            r1[o, i].wait_recv()
            block = (gat[o] + side[i]) % RING
            rows = pl.ds(i * half, half)
            gb[o, block, rows, :] = gb[o, block, rows, :] + load_code(rh.at[o, i])
            hand(o, i, i)

    w1, w2 = {}, {}

    def weights(o):
        for part in range(2):
            for i in range(2):
                h = halves(i)[part]
                rows = wb.at[o, gat[o], h]
                w1[o, i, h] = send(rows, rows, S_W1 + 4 * o + 2 * i + h, along_gather(o, side[i]))

    def forward(o):
        for i in range(2):
            w1[o, i, i].wait_recv()
            rows = wb.at[o, (gat[o] + RING - side[i]) % RING, i]
            w2[o, i] = send(rows, rows, S_W2 + 2 * o + i, along_gather(o, side[i]))

    weights(0)
    for copy in wz:
        copy.wait_recv()
    weights(1)
    for o in (1, 0):
        partial(o, 0)

    for copy in ins:
        copy.wait()
    mine = pl.ds(pl.multiple_of(worker * PART, 8), PART)
    anchor = fav[mine, :]
    total = anchor - fr[0]
    for j in range(1, WORKERS):
        loc[j - 1].wait_recv()
        total = total + (anchor - fr[j])
    ps[mine, :] = total
    pse = [send(ps.at[mine], ps.at[mine], S_PSE + j - 1, other_worker(j)) for j in range(1, WORKERS)]

    def plane(o):
        for i in range(2):
            for h in range(2):
                r2[o, i, h].wait_recv()
        for h in range(2):
            rows = pl.ds(h * half, half)
            gb[o, gat[o], rows, :] = gb[o, gat[o], rows, :] + load_code(rf.at[o, 0, h]) + load_code(rf.at[o, 1, h])

    plane(1)
    gz = [
        send(code_of(gs.at[h], gb[1, gat[1], pl.ds(h * half, half), :]), zr.at[h], S_GZ + h, partner)
        for h in range(2)
    ]
    forward(0)
    forward(1)
    give(0, gat[0], 0)

    product(1, 0)
    for i in range(2):
        for o in range(2):
            w1[o, 1 - i, i].wait_recv()
            product(o, side[i])
    plane(0)
    for o in range(2):
        for i in range(2):
            w2[o, i].wait_recv()
        product(o, 2)

    for copy in pse:
        copy.wait_recv()
    pseudo = ps[...] / WORKERS
    momentum = outer_mass * omv[...] + pseudo
    nmv[...] = momentum
    nav[...] = fav[...] - outer_rate * (pseudo + outer_mass * momentum)
    results = [local(nmv, nm_ref, L_RES), local(nav, na_ref, L_RES + 1)]

    for h in range(2):
        gz[h].wait_recv()
        rows = pl.ds(h * half, half)
        gradient = gb[0, gat[0], rows, :] + load_code(zr.at[h])
        weight = wv[rows, :]
        first_new = first_decay * fmv[rows, :] + (1.0 - first_decay) * gradient
        second_new = second_decay * smv[rows, :] + (1.0 - second_decay) * gradient * gradient
        first_hat = first_new / (1.0 - first_decay**adam_count)
        second_hat = second_new / (1.0 - second_decay**adam_count)
        nfv[rows, :] = first_new
        nsv[rows, :] = second_new
        nwv[rows, :] = weight - inner_rate * (
            first_hat / (jnp.sqrt(second_hat) + adam_epsilon) + weight_decay * weight
        )
    results += [local(nfv, nf_ref, L_RES + 2), local(nsv, ns_ref, L_RES + 3), local(nwv, nw_ref, L_RES + 4)]

    for copy in out:
        copy.wait_recv()
    for copy in results + out_here:
        copy.wait()
    for copy in sent:
        copy.wait_send()


GROUP = 4


def finish(code_ref, *refs):
    fg_ref = refs[5]
    code, wide, stage, sems = refs[11:]
    groups = code_ref.shape[0] // GROUP
    loads = [
        pltpu.make_async_copy(code_ref.at[pl.ds(i * GROUP, GROUP)], code.at[pl.ds(i * GROUP, GROUP)], sems.at[0, i])
        for i in range(groups)
    ]
    stores = [
        pltpu.make_async_copy(
            wide.at[:, pl.ds(i * GROUP * ROWS, GROUP * ROWS)],
            fg_ref.at[:, pl.ds(i * GROUP * ROWS, GROUP * ROWS)],
            sems.at[1, i],
        )
        for i in range(groups)
    ]
    into = [pltpu.make_async_copy(refs[k], stage.at[k], sems.at[0, groups + k]) for k in range(5)]
    outof = [pltpu.make_async_copy(stage.at[k], refs[6 + k], sems.at[1, groups + k]) for k in range(5)]
    for copy in loads + into:
        copy.start()
    for i in range(groups):
        loads[i].wait()
        for k in range(i * GROUP, (i + 1) * GROUP):
            wide[:, pl.ds(k * ROWS, ROWS)] = load_code(code.at[k])
        stores[i].start()
        if i == groups - 2:
            for load, store in zip(into, outof):
                load.wait()
                store.start()
    for copy in stores + outof:
        copy.wait()


def on_device(
    features, value_cotangent, value_weight, first_moment, second_moment, fragment_local, fragment_anchor,
    outer_momentum,
):
    hbm = pl.BlockSpec(memory_space=pltpu.HBM)
    slabs = features.shape[1] // ROWS
    param = jax.ShapeDtypeStruct((ROWS, COLS), F32)
    vparam = pltpu.VMEM((ROWS, COLS), F32)
    got = pl.pallas_call(
        kernel,
        name="backward",
        out_shape=(jax.ShapeDtypeStruct((slabs, TOK + MARK, ROWS), BF16),) + (param,) * 5,
        in_specs=[hbm] * 8,
        out_specs=(hbm,) * 6,
        scratch_shapes=[
            pltpu.VMEM((2, RING, RING * TOK, ROWS), BF16),
            pltpu.VMEM((2, RING * TOK, COLS), BF16),
            pltpu.VMEM((2, RING, 2, ROWS // 2 + MARK, COLS), BF16),
            pltpu.VMEM((2, RING, ROWS, COLS), F32),
            pltpu.VMEM((2, 2, ROWS // 2 + MARK, COLS), BF16),
            pltpu.VMEM((2, 2, ROWS // 2 + MARK, COLS), BF16),
            pltpu.VMEM((2, 2, 2, ROWS // 2 + MARK, COLS), BF16),
            pltpu.VMEM((2, 2, 2, ROWS // 2 + MARK, COLS), BF16),
            pltpu.VMEM((2, ROWS // 2 + MARK, COLS), BF16),
            pltpu.VMEM((2, ROWS // 2 + MARK, COLS), BF16),
            pltpu.VMEM((2, RING, RING, TOK + MARK, ROWS), BF16),
            pltpu.VMEM((ROWS, COLS), BF16),
            pltpu.VMEM((ROWS, COLS), BF16),
            vparam, vparam, vparam, vparam, vparam,
            pltpu.VMEM((WORKERS, PART, COLS), F32),
            vparam,
            vparam, vparam, vparam, vparam, vparam,
            pltpu.SemaphoreType.DMA((N_REMOTE,)),
            pltpu.SemaphoreType.DMA((N_REMOTE,)),
            pltpu.SemaphoreType.DMA((N_LOCAL,)),
        ],
        compiler_params=pltpu.CompilerParams(
            collective_id=0, has_side_effects=True, vmem_limit_bytes=56 * 2**20
        ),
    )(
        features, value_cotangent, value_weight[0], first_moment[0], second_moment[0], fragment_local[0],
        fragment_anchor, outer_momentum,
    )
    feature_grad, weight_new, first_new, second_new, new_anchor, new_momentum = pl.pallas_call(
        finish,
        name="finish",
        out_shape=(jax.ShapeDtypeStruct(features.shape, F32),) + (param,) * 5,
        in_specs=[hbm] * 6,
        out_specs=(hbm,) * 6,
        scratch_shapes=[
            pltpu.VMEM((slabs, TOK + MARK, ROWS), BF16),
            pltpu.VMEM(features.shape, F32),
            pltpu.VMEM((5, ROWS, COLS), F32),
            pltpu.SemaphoreType.DMA((2, slabs // GROUP + 5)),
        ],
        compiler_params=pltpu.CompilerParams(vmem_limit_bytes=60 * 2**20),
    )(*got)
    return feature_grad, weight_new[None], first_new[None], second_new[None], new_anchor, new_momentum


def solution(mesh):
    tokens = P(("worker", "fsdp"), None)
    groups = P("worker", "fsdp", None)
    whole = P("fsdp", None)
    return jax.shard_map(
        on_device,
        mesh=mesh,
        in_specs=(tokens, tokens, groups, groups, groups, groups, whole, whole),
        out_specs=(tokens, groups, groups, groups, whole, whole),
        check_vma=False,
    )
```

```python
import jax
import jax.numpy as jnp
from jax import lax
from jax.experimental import pallas as pl
from jax.experimental.pallas import tpu as pltpu
from jax.sharding import PartitionSpec as P

MESH = pl.DeviceIdType.MESH
F32 = jnp.float32
BF16 = jnp.bfloat16

first_decay = 0.9
second_decay = 0.95
inner_rate = 0.001
weight_decay = 0.1
adam_epsilon = 1e-08
adam_count = 10.0
outer_rate = 0.7
outer_mass = 0.9

RING = 4
TOK = 192
ROWS = 256
COLS = 512
WORKERS = 8
PART = ROWS // WORKERS

_count = 0


def _take(n):
    global _count
    base = _count
    _count += n
    return base


S_FEAT = _take(2 * 3 * RING)
S_COT1 = _take(8)
S_COT2 = _take(4)
S_WZ = _take(2)
S_W1 = _take(8)
S_W2 = _take(4)
S_R1 = _take(4)
S_R2 = _take(8)
S_GZ = _take(2)
S_OUT = _take(2 * 3 * RING)
S_LOC = _take(WORKERS - 1)
S_PSE = _take(WORKERS - 1)
N_REMOTE = _count

L_FEAT = 0
L_COT = 8
L_W = 10
L_IN = 11
L_OUT = 17
L_RES = 25
N_LOCAL = 30

STEPS = 30847.0
MARK = 8


def encode(t):
    largest = jnp.max(jnp.abs(t), axis=0, keepdims=True)
    unit = jnp.maximum(largest * 1.01, 1e-30).astype(BF16).astype(F32)
    q = t * (STEPS / unit)
    n = jnp.minimum(jnp.floor(jnp.abs(q) + 0.5), STEPS)
    e = jnp.floor(n * (1.0 / 128.0))
    size = (1.0 + (n - 128.0 * e) * (1.0 / 128.0)) * jnp.exp2(e - 120.0)
    return jnp.where(q < 0, -size, size).astype(BF16), unit


def store_code(ref, t):
    code, unit = encode(t)
    rows = t.shape[0]
    ref[pl.ds(0, rows), :] = code
    ref[pl.ds(rows, MARK), :] = jnp.broadcast_to(unit, (MARK, t.shape[1])).astype(BF16)


def code_of(ref, t):
    store_code(ref, t)
    return ref


def load_code(ref):
    rows = ref.shape[0] - MARK
    unit = ref[pl.ds(rows, MARK), :].astype(F32)[0:1]
    return decode(ref[pl.ds(0, rows), :], unit)


def decode(code, unit):
    v = code.astype(F32)
    a = jnp.abs(v)
    e = jnp.floor(jnp.log(a) * 1.4426950408889634 + 0.0025)
    n = jnp.floor(a * jnp.exp2(7.0 - e) + 0.5) + (e * 128.0 + 119.0 * 128.0)
    n = n * (unit * (1.0 / STEPS))
    return jnp.where(v < 0, -n, n)


def kernel(
    f_ref, c_ref, w_ref, fm_ref, sm_ref, fl_ref, fa_ref, om_ref,
    code_ref, nw_ref, nf_ref, ns_ref, na_ref, nm_ref,
    fb, cb, wb, gb, r1s, rh, r2s, rf, gs, zr, ob, high, low, wv, fmv, smv, fav, omv, fr, ps,
    nwv, nfv, nsv, nav, nmv,
    ssem, rsem, lsem,
):
    worker = lax.axis_index("worker")
    place = lax.axis_index("fsdp")
    x, y, zh = place // 8, (place // 2) % RING, place % 2

    zo = (zh, 1 - zh)
    gat = tuple(x * (1 - z) + y * z for z in zo)
    exc = tuple(y * (1 - z) + x * z for z in zo)

    def along_gather(o, d):
        z = zo[o]
        xx, yy = (x + d * (1 - z)) % RING, (y + d * z) % RING
        return (worker, (xx * RING + yy) * 2 + zh)

    def along_exchange(o, d):
        z = zo[o]
        xx, yy = (x + d * z) % RING, (y + d * (1 - z)) % RING
        return (worker, (xx * RING + yy) * 2 + zh)

    partner = (worker, place + 1 - 2 * zh)

    def other_worker(j):
        return ((worker + j) % WORKERS, place)

    def column(o, g, e):
        z = zo[o]
        start = g * (2048 - 1536 * z) + e * (512 + 1536 * z) + z * ROWS
        return pl.ds(pl.multiple_of(start, ROWS), ROWS)

    def slab(o, g, e):
        z = zo[o]
        return g * (8 - 6 * z) + e * (2 + 6 * z) + z

    def tokens(e, half=None):
        if half is None:
            return pl.ds(pl.multiple_of(e * TOK, 16), TOK)
        return pl.ds(pl.multiple_of(e * TOK + half * (TOK // 2), 16), TOK // 2)

    sent = []

    def send(src, dst, sem, device):
        copy = pltpu.make_async_remote_copy(
            src_ref=src, dst_ref=dst, send_sem=ssem.at[sem], recv_sem=rsem.at[sem],
            device_id=device, device_id_type=MESH,
        )
        copy.start()
        sent.append(copy)
        return copy

    def local(src, dst, sem):
        copy = pltpu.make_async_copy(src, dst, lsem.at[sem])
        copy.start()
        return copy

    barrier = pltpu.get_barrier_semaphore()
    peers = [along_gather(0, d) for d in (1, 2, 3)] + [along_exchange(0, d) for d in (1, 2, 3)]
    peers += [partner] + [other_worker(j) for j in range(1, WORKERS)]
    for peer in peers:
        pl.semaphore_signal(barrier, inc=1, device_id=peer, device_id_type=MESH)

    w_here = local(w_ref, wv, L_W)
    cot_here = [local(c_ref, cb.at[o, tokens(exc[o])], L_COT + o) for o in range(2)]
    feat_here = [
        local(f_ref.at[:, column(o, g, exc[o])], fb.at[o, g, tokens(exc[o])], L_FEAT + o * RING + g)
        for o in range(2)
        for g in range(RING)
    ]
    ins = [
        local(src, dst, L_IN + i)
        for i, (src, dst) in enumerate(
            ((fm_ref, fmv), (sm_ref, smv), (fa_ref, fav), (om_ref, omv),
             (fl_ref.at[pl.ds(pl.multiple_of(worker * PART, 8), PART)], fr.at[0]))
        )
    ]
    half = ROWS // 2
    w_here.wait()
    for h in range(2):
        store_code(wb.at[0, gat[0], h], wv[pl.ds(h * half, half), :])
    pl.semaphore_wait(barrier, len(peers))

    side = (1, RING - 1)

    def halves(i):
        return (i, 1 - i)

    cot1 = {}
    for part in range(2):
        for o in range(2):
            for i in range(2):
                h = halves(i)[part]
                cot1[o, i, h] = send(
                    c_ref.at[pl.ds(h * (TOK // 2), TOK // 2)], cb.at[o, tokens(exc[o], h)],
                    S_COT1 + 4 * o + 2 * i + h, along_exchange(o, side[i]),
                )
    wz = [send(wb.at[0, gat[0], h], wb.at[1, gat[0], h], S_WZ + h, partner) for h in range(2)]
    feat = {}

    def features(at):
        for d in (2, 1, 3):
            for o in range(2):
                feat[o, at, d] = send(
                    f_ref.at[:, column(o, (gat[o] + at) % RING, (exc[o] + d) % RING)],
                    fb.at[o, (gat[o] + at) % RING, tokens(exc[o])],
                    S_FEAT + (o * 3 + d - 1) * RING + at,
                    along_exchange(o, d),
                )

    features(2)

    for copy in cot_here:
        copy.wait()
    cot2 = []
    for o in range(2):
        for i in range(2):
            cot1[o, i, i].wait_recv()
            rows = cb.at[o, tokens((exc[o] + RING - side[i]) % RING, i)]
            cot2.append(send(rows, rows, S_COT2 + 2 * o + i, along_exchange(o, side[i])))
    for at in (1, 3, 0):
        features(at)
    loc = [
        send(
            fl_ref.at[pl.ds(pl.multiple_of((worker + j) % WORKERS * PART, 8), PART)],
            fr.at[j], S_LOC + j - 1, other_worker(j),
        )
        for j in range(1, WORKERS)
    ]

    def multiply(o, g):
        for h in range(2):
            w = load_code(wb.at[o, g, h])
            top = w.astype(BF16)
            high[pl.ds(h * half, half), :] = top
            low[pl.ds(h * half, half), :] = (w - top.astype(F32)).astype(BF16)
        dims = (((1,), (1,)), ((), ()))

        def step(e, carry):
            c = cb[o, tokens(e)]
            t = lax.dot_general(c, high[...], dims, preferred_element_type=F32) + lax.dot_general(
                c, low[...], dims, preferred_element_type=F32
            )
            store_code(ob.at[o, g, e], t)
            return carry

        lax.fori_loop(0, RING, step, 0)

    out = []
    out_here = []

    def give(o, g, at):
        there = code_ref.at[slab(o, g, exc[o])]
        for d in (2, 1, 3):
            out.append(
                send(
                    ob.at[o, g, (exc[o] + d) % RING], there,
                    S_OUT + (o * 3 + d - 1) * RING + at, along_exchange(o, d),
                )
            )
        out_here.append(local(ob.at[o, g, exc[o]], there, L_OUT + o * RING + at))

    def product(o, at):
        g = (gat[o] + at) % RING
        multiply(o, g)
        give(o, g, at)

    for copy in feat_here:
        copy.wait()
    for key in cot1:
        if key[1] != key[2]:
            cot1[key].wait_recv()
    for copy in cot2:
        copy.wait_recv()
    multiply(0, gat[0])

    def partial(o, at):
        g = (gat[o] + at) % RING
        for d in (2, 1, 3):
            feat[o, at, d].wait_recv()
        gb[o, g] = lax.dot_general(
            fb[o, g], cb[o], (((0,), (0,)), ((), ())), preferred_element_type=F32
        )

    r1, r2 = {}, {}
    for o in range(2):
        far = (gat[o] + 2) % RING
        partial(o, 2)
        for i in range(2):
            r1[o, i] = send(
                code_of(r1s.at[o, i], gb[o, far, pl.ds(i * half, half), :]), rh.at[o, i],
                S_R1 + 2 * o + i, along_gather(o, side[i]),
            )

    def hand(o, i, h):
        block = (gat[o] + side[i]) % RING
        r2[o, i, h] = send(
            code_of(r2s.at[o, i, h], gb[o, block, pl.ds(h * half, half), :]), rf.at[o, i, h],
            S_R2 + 4 * o + 2 * i + h, along_gather(o, side[i]),
        )

    for i in range(2):
        for o in range(2):
            partial(o, side[i])
            hand(o, i, 1 - i)
    for o in range(2):
        for i in range(2):
            r1[o, i].wait_recv()
            block = (gat[o] + side[i]) % RING
            rows = pl.ds(i * half, half)
            gb[o, block, rows, :] = gb[o, block, rows, :] + load_code(rh.at[o, i])
            hand(o, i, i)

    w1, w2 = {}, {}

    def weights(o):
        for part in range(2):
            for i in range(2):
                h = halves(i)[part]
                rows = wb.at[o, gat[o], h]
                w1[o, i, h] = send(rows, rows, S_W1 + 4 * o + 2 * i + h, along_gather(o, side[i]))

    def forward(o):
        for i in range(2):
            w1[o, i, i].wait_recv()
            rows = wb.at[o, (gat[o] + RING - side[i]) % RING, i]
            w2[o, i] = send(rows, rows, S_W2 + 2 * o + i, along_gather(o, side[i]))

    weights(0)
    for copy in wz:
        copy.wait_recv()
    weights(1)
    for o in (1, 0):
        partial(o, 0)

    for copy in ins:
        copy.wait()
    mine = pl.ds(pl.multiple_of(worker * PART, 8), PART)
    anchor = fav[mine, :]
    total = anchor - fr[0]
    for j in range(1, WORKERS):
        loc[j - 1].wait_recv()
        total = total + (anchor - fr[j])
    ps[mine, :] = total
    pse = [send(ps.at[mine], ps.at[mine], S_PSE + j - 1, other_worker(j)) for j in range(1, WORKERS)]

    def plane(o):
        for i in range(2):
            for h in range(2):
                r2[o, i, h].wait_recv()
        for h in range(2):
            rows = pl.ds(h * half, half)
            gb[o, gat[o], rows, :] = gb[o, gat[o], rows, :] + load_code(rf.at[o, 0, h]) + load_code(rf.at[o, 1, h])

    plane(1)
    gz = [
        send(code_of(gs.at[h], gb[1, gat[1], pl.ds(h * half, half), :]), zr.at[h], S_GZ + h, partner)
        for h in range(2)
    ]
    forward(0)
    forward(1)
    give(0, gat[0], 0)

    product(1, 0)
    for i in range(2):
        for o in range(2):
            w1[o, 1 - i, i].wait_recv()
            product(o, side[i])
    plane(0)
    for o in range(2):
        for i in range(2):
            w2[o, i].wait_recv()
        product(o, 2)

    for copy in pse:
        copy.wait_recv()
    pseudo = ps[...] / WORKERS
    momentum = outer_mass * omv[...] + pseudo
    nmv[...] = momentum
    nav[...] = fav[...] - outer_rate * (pseudo + outer_mass * momentum)
    results = [local(nmv, nm_ref, L_RES), local(nav, na_ref, L_RES + 1)]

    for h in range(2):
        gz[h].wait_recv()
        rows = pl.ds(h * half, half)
        gradient = gb[0, gat[0], rows, :] + load_code(zr.at[h])
        weight = wv[rows, :]
        first_new = first_decay * fmv[rows, :] + (1.0 - first_decay) * gradient
        second_new = second_decay * smv[rows, :] + (1.0 - second_decay) * gradient * gradient
        first_hat = first_new / (1.0 - first_decay**adam_count)
        second_hat = second_new / (1.0 - second_decay**adam_count)
        nfv[rows, :] = first_new
        nsv[rows, :] = second_new
        nwv[rows, :] = weight - inner_rate * (
            first_hat / (jnp.sqrt(second_hat) + adam_epsilon) + weight_decay * weight
        )
    results += [local(nfv, nf_ref, L_RES + 2), local(nsv, ns_ref, L_RES + 3), local(nwv, nw_ref, L_RES + 4)]

    for copy in out:
        copy.wait_recv()
    for copy in results + out_here:
        copy.wait()
    for copy in sent:
        copy.wait_send()


GROUP = 4


def finish(code_ref, *refs):
    fg_ref = refs[5]
    code, wide, stage, sems = refs[11:]
    groups = code_ref.shape[0] // GROUP
    loads = [
        pltpu.make_async_copy(code_ref.at[pl.ds(i * GROUP, GROUP)], code.at[pl.ds(i * GROUP, GROUP)], sems.at[0, i])
        for i in range(groups)
    ]
    stores = [
        pltpu.make_async_copy(
            wide.at[:, pl.ds(i * GROUP * ROWS, GROUP * ROWS)],
            fg_ref.at[:, pl.ds(i * GROUP * ROWS, GROUP * ROWS)],
            sems.at[1, i],
        )
        for i in range(groups)
    ]
    into = [pltpu.make_async_copy(refs[k], stage.at[k], sems.at[0, groups + k]) for k in range(5)]
    outof = [pltpu.make_async_copy(stage.at[k], refs[6 + k], sems.at[1, groups + k]) for k in range(5)]
    for copy in loads + into:
        copy.start()
    for i in range(groups):
        loads[i].wait()
        for k in range(i * GROUP, (i + 1) * GROUP):
            wide[:, pl.ds(k * ROWS, ROWS)] = load_code(code.at[k])
        stores[i].start()
        if i == groups - 2:
            for load, store in zip(into, outof):
                load.wait()
                store.start()
    for copy in stores + outof:
        copy.wait()


def on_device(
    features, value_cotangent, value_weight, first_moment, second_moment, fragment_local, fragment_anchor,
    outer_momentum,
):
    hbm = pl.BlockSpec(memory_space=pltpu.HBM)
    slabs = features.shape[1] // ROWS
    param = jax.ShapeDtypeStruct((ROWS, COLS), F32)
    vparam = pltpu.VMEM((ROWS, COLS), F32)
    got = pl.pallas_call(
        kernel,
        name="backward",
        out_shape=(jax.ShapeDtypeStruct((slabs, TOK + MARK, ROWS), BF16),) + (param,) * 5,
        in_specs=[hbm] * 8,
        out_specs=(hbm,) * 6,
        scratch_shapes=[
            pltpu.VMEM((2, RING, RING * TOK, ROWS), BF16),
            pltpu.VMEM((2, RING * TOK, COLS), BF16),
            pltpu.VMEM((2, RING, 2, ROWS // 2 + MARK, COLS), BF16),
            pltpu.VMEM((2, RING, ROWS, COLS), F32),
            pltpu.VMEM((2, 2, ROWS // 2 + MARK, COLS), BF16),
            pltpu.VMEM((2, 2, ROWS // 2 + MARK, COLS), BF16),
            pltpu.VMEM((2, 2, 2, ROWS // 2 + MARK, COLS), BF16),
            pltpu.VMEM((2, 2, 2, ROWS // 2 + MARK, COLS), BF16),
            pltpu.VMEM((2, ROWS // 2 + MARK, COLS), BF16),
            pltpu.VMEM((2, ROWS // 2 + MARK, COLS), BF16),
            pltpu.VMEM((2, RING, RING, TOK + MARK, ROWS), BF16),
            pltpu.VMEM((ROWS, COLS), BF16),
            pltpu.VMEM((ROWS, COLS), BF16),
            vparam, vparam, vparam, vparam, vparam,
            pltpu.VMEM((WORKERS, PART, COLS), F32),
            vparam,
            vparam, vparam, vparam, vparam, vparam,
            pltpu.SemaphoreType.DMA((N_REMOTE,)),
            pltpu.SemaphoreType.DMA((N_REMOTE,)),
            pltpu.SemaphoreType.DMA((N_LOCAL,)),
        ],
        compiler_params=pltpu.CompilerParams(
            collective_id=0, has_side_effects=True, vmem_limit_bytes=56 * 2**20
        ),
    )(
        features, value_cotangent, value_weight[0], first_moment[0], second_moment[0], fragment_local[0],
        fragment_anchor, outer_momentum,
    )
    feature_grad, weight_new, first_new, second_new, new_anchor, new_momentum = pl.pallas_call(
        finish,
        name="finish",
        out_shape=(jax.ShapeDtypeStruct(features.shape, F32),) + (param,) * 5,
        in_specs=[hbm] * 6,
        out_specs=(hbm,) * 6,
        scratch_shapes=[
            pltpu.VMEM((slabs, TOK + MARK, ROWS), BF16),
            pltpu.VMEM(features.shape, F32),
            pltpu.VMEM((5, ROWS, COLS), F32),
            pltpu.SemaphoreType.DMA((2, slabs // GROUP + 5)),
        ],
        compiler_params=pltpu.CompilerParams(vmem_limit_bytes=60 * 2**20),
    )(*got)
    return feature_grad, weight_new[None], first_new[None], second_new[None], new_anchor, new_momentum


def solution(mesh):
    tokens = P(("worker", "fsdp"), None)
    groups = P("worker", "fsdp", None)
    whole = P("fsdp", None)
    return jax.shard_map(
        on_device,
        mesh=mesh,
        in_specs=(tokens, tokens, groups, groups, groups, groups, whole, whole),
        out_specs=(tokens, groups, groups, groups, whole, whole),
        check_vma=False,
    )
```

```python
import jax
import jax.numpy as jnp
from jax import lax
from jax.experimental import pallas as pl
from jax.experimental.pallas import tpu as pltpu
from jax.sharding import PartitionSpec as P

MESH = pl.DeviceIdType.MESH
F32 = jnp.float32
BF16 = jnp.bfloat16

first_decay = 0.9
second_decay = 0.95
inner_rate = 0.001
weight_decay = 0.1
adam_epsilon = 1e-08
adam_count = 10.0
outer_rate = 0.7
outer_mass = 0.9

RING = 4
TOK = 192
ROWS = 256
COLS = 512
WORKERS = 8
PART = ROWS // WORKERS

_count = 0


def _take(n):
    global _count
    base = _count
    _count += n
    return base


S_FEAT = _take(2 * 3 * RING)
S_COT1 = _take(8)
S_COT2 = _take(4)
S_WZ = _take(2)
S_W1 = _take(8)
S_W2 = _take(4)
S_R1 = _take(4)
S_R2 = _take(8)
S_GZ = _take(2)
S_OUT = _take(2 * 3 * RING)
S_LOC = _take(WORKERS - 1)
S_PSE = _take(WORKERS - 1)
N_REMOTE = _count

L_FEAT = 0
L_COT = 8
L_W = 10
L_IN = 11
L_OUT = 17
L_RES = 25
N_LOCAL = 30

STEPS = 30847.0
MARK = 8


def encode(t):
    largest = jnp.max(jnp.abs(t), axis=0, keepdims=True)
    unit = jnp.maximum(largest * 1.01, 1e-30).astype(BF16).astype(F32)
    q = t * (STEPS / unit)
    n = jnp.minimum(jnp.floor(jnp.abs(q) + 0.5), STEPS)
    e = jnp.floor(n * (1.0 / 128.0))
    size = (1.0 + (n - 128.0 * e) * (1.0 / 128.0)) * jnp.exp2(e - 120.0)
    return jnp.where(q < 0, -size, size).astype(BF16), unit


def store_code(ref, t):
    code, unit = encode(t)
    rows = t.shape[0]
    ref[pl.ds(0, rows), :] = code
    ref[pl.ds(rows, MARK), :] = jnp.broadcast_to(unit, (MARK, t.shape[1])).astype(BF16)


def code_of(ref, t):
    store_code(ref, t)
    return ref


def load_code(ref):
    rows = ref.shape[0] - MARK
    unit = ref[pl.ds(rows, MARK), :].astype(F32)[0:1]
    return decode(ref[pl.ds(0, rows), :], unit)


def decode(code, unit):
    v = code.astype(F32)
    a = jnp.abs(v)
    e = jnp.floor(jnp.log(a) * 1.4426950408889634 + 0.0025)
    n = a * jnp.exp2(7.0 - e) + (e * 128.0 + 119.0 * 128.0)
    step = unit * (1.0 / STEPS)
    return n * jnp.where(v < 0, -step, step)


def kernel(
    f_ref, c_ref, w_ref, fm_ref, sm_ref, fl_ref, fa_ref, om_ref,
    code_ref, nw_ref, nf_ref, ns_ref, na_ref, nm_ref,
    fb, cb, wb, gb, r1s, rh, r2s, rf, gs, zr, ob, high, low, wv, fmv, smv, fav, omv, fr, ps,
    nwv, nfv, nsv, nav, nmv,
    ssem, rsem, lsem,
):
    worker = lax.axis_index("worker")
    place = lax.axis_index("fsdp")
    x, y, zh = place // 8, (place // 2) % RING, place % 2

    zo = (zh, 1 - zh)
    gat = tuple(x * (1 - z) + y * z for z in zo)
    exc = tuple(y * (1 - z) + x * z for z in zo)

    def along_gather(o, d):
        z = zo[o]
        xx, yy = (x + d * (1 - z)) % RING, (y + d * z) % RING
        return (worker, (xx * RING + yy) * 2 + zh)

    def along_exchange(o, d):
        z = zo[o]
        xx, yy = (x + d * z) % RING, (y + d * (1 - z)) % RING
        return (worker, (xx * RING + yy) * 2 + zh)

    partner = (worker, place + 1 - 2 * zh)

    def other_worker(j):
        return ((worker + j) % WORKERS, place)

    def column(o, g, e):
        z = zo[o]
        start = g * (2048 - 1536 * z) + e * (512 + 1536 * z) + z * ROWS
        return pl.ds(pl.multiple_of(start, ROWS), ROWS)

    def slab(o, g, e):
        z = zo[o]
        return g * (8 - 6 * z) + e * (2 + 6 * z) + z

    def tokens(e, half=None):
        if half is None:
            return pl.ds(pl.multiple_of(e * TOK, 16), TOK)
        return pl.ds(pl.multiple_of(e * TOK + half * (TOK // 2), 16), TOK // 2)

    sent = []

    def send(src, dst, sem, device):
        copy = pltpu.make_async_remote_copy(
            src_ref=src, dst_ref=dst, send_sem=ssem.at[sem], recv_sem=rsem.at[sem],
            device_id=device, device_id_type=MESH,
        )
        copy.start()
        sent.append(copy)
        return copy

    def local(src, dst, sem):
        copy = pltpu.make_async_copy(src, dst, lsem.at[sem])
        copy.start()
        return copy

    barrier = pltpu.get_barrier_semaphore()
    peers = [along_gather(0, d) for d in (1, 2, 3)] + [along_exchange(0, d) for d in (1, 2, 3)]
    peers += [partner] + [other_worker(j) for j in range(1, WORKERS)]
    for peer in peers:
        pl.semaphore_signal(barrier, inc=1, device_id=peer, device_id_type=MESH)

    w_here = local(w_ref, wv, L_W)
    cot_here = [local(c_ref, cb.at[o, tokens(exc[o])], L_COT + o) for o in range(2)]
    feat_here = [
        local(f_ref.at[:, column(o, g, exc[o])], fb.at[o, g, tokens(exc[o])], L_FEAT + o * RING + g)
        for o in range(2)
        for g in range(RING)
    ]
    ins = [
        local(src, dst, L_IN + i)
        for i, (src, dst) in enumerate(
            ((fm_ref, fmv), (sm_ref, smv), (fa_ref, fav), (om_ref, omv),
             (fl_ref.at[pl.ds(pl.multiple_of(worker * PART, 8), PART)], fr.at[0]))
        )
    ]
    half = ROWS // 2
    w_here.wait()
    for h in range(2):
        store_code(wb.at[0, gat[0], h], wv[pl.ds(h * half, half), :])
    pl.semaphore_wait(barrier, len(peers))

    side = (1, RING - 1)

    def halves(i):
        return (i, 1 - i)

    cot1 = {}
    for part in range(2):
        for o in range(2):
            for i in range(2):
                h = halves(i)[part]
                cot1[o, i, h] = send(
                    c_ref.at[pl.ds(h * (TOK // 2), TOK // 2)], cb.at[o, tokens(exc[o], h)],
                    S_COT1 + 4 * o + 2 * i + h, along_exchange(o, side[i]),
                )
    wz = [send(wb.at[0, gat[0], h], wb.at[1, gat[0], h], S_WZ + h, partner) for h in range(2)]
    feat = {}

    def features(at):
        for d in (2, 1, 3):
            for o in range(2):
                feat[o, at, d] = send(
                    f_ref.at[:, column(o, (gat[o] + at) % RING, (exc[o] + d) % RING)],
                    fb.at[o, (gat[o] + at) % RING, tokens(exc[o])],
                    S_FEAT + (o * 3 + d - 1) * RING + at,
                    along_exchange(o, d),
                )

    features(2)

    for copy in cot_here:
        copy.wait()
    cot2 = []
    for o in range(2):
        for i in range(2):
            cot1[o, i, i].wait_recv()
            rows = cb.at[o, tokens((exc[o] + RING - side[i]) % RING, i)]
            cot2.append(send(rows, rows, S_COT2 + 2 * o + i, along_exchange(o, side[i])))
    for at in (1, 3, 0):
        features(at)
    loc = [
        send(
            fl_ref.at[pl.ds(pl.multiple_of((worker + j) % WORKERS * PART, 8), PART)],
            fr.at[j], S_LOC + j - 1, other_worker(j),
        )
        for j in range(1, WORKERS)
    ]

    def multiply(o, g):
        for h in range(2):
            w = load_code(wb.at[o, g, h])
            top = w.astype(BF16)
            high[pl.ds(h * half, half), :] = top
            low[pl.ds(h * half, half), :] = (w - top.astype(F32)).astype(BF16)
        dims = (((1,), (1,)), ((), ()))

        def step(e, carry):
            c = cb[o, tokens(e)]
            t = lax.dot_general(c, high[...], dims, preferred_element_type=F32) + lax.dot_general(
                c, low[...], dims, preferred_element_type=F32
            )
            store_code(ob.at[o, g, e], t)
            return carry

        lax.fori_loop(0, RING, step, 0)

    out = []
    out_here = []

    def give(o, g, at):
        there = code_ref.at[slab(o, g, exc[o])]
        for d in (2, 1, 3):
            out.append(
                send(
                    ob.at[o, g, (exc[o] + d) % RING], there,
                    S_OUT + (o * 3 + d - 1) * RING + at, along_exchange(o, d),
                )
            )
        out_here.append(local(ob.at[o, g, exc[o]], there, L_OUT + o * RING + at))

    def product(o, at):
        g = (gat[o] + at) % RING
        multiply(o, g)
        give(o, g, at)

    for copy in feat_here:
        copy.wait()
    for key in cot1:
        if key[1] != key[2]:
            cot1[key].wait_recv()
    for copy in cot2:
        copy.wait_recv()
    multiply(0, gat[0])

    def partial(o, at):
        g = (gat[o] + at) % RING
        for d in (2, 1, 3):
            feat[o, at, d].wait_recv()
        gb[o, g] = lax.dot_general(
            fb[o, g], cb[o], (((0,), (0,)), ((), ())), preferred_element_type=F32
        )

    r1, r2 = {}, {}
    for o in range(2):
        far = (gat[o] + 2) % RING
        partial(o, 2)
        for i in range(2):
            r1[o, i] = send(
                code_of(r1s.at[o, i], gb[o, far, pl.ds(i * half, half), :]), rh.at[o, i],
                S_R1 + 2 * o + i, along_gather(o, side[i]),
            )

    def hand(o, i, h):
        block = (gat[o] + side[i]) % RING
        r2[o, i, h] = send(
            code_of(r2s.at[o, i, h], gb[o, block, pl.ds(h * half, half), :]), rf.at[o, i, h],
            S_R2 + 4 * o + 2 * i + h, along_gather(o, side[i]),
        )

    for i in range(2):
        for o in range(2):
            partial(o, side[i])
            hand(o, i, 1 - i)
    for o in range(2):
        for i in range(2):
            r1[o, i].wait_recv()
            block = (gat[o] + side[i]) % RING
            rows = pl.ds(i * half, half)
            gb[o, block, rows, :] = gb[o, block, rows, :] + load_code(rh.at[o, i])
            hand(o, i, i)

    w1, w2 = {}, {}

    def weights(o):
        for part in range(2):
            for i in range(2):
                h = halves(i)[part]
                rows = wb.at[o, gat[o], h]
                w1[o, i, h] = send(rows, rows, S_W1 + 4 * o + 2 * i + h, along_gather(o, side[i]))

    def forward(o):
        for i in range(2):
            w1[o, i, i].wait_recv()
            rows = wb.at[o, (gat[o] + RING - side[i]) % RING, i]
            w2[o, i] = send(rows, rows, S_W2 + 2 * o + i, along_gather(o, side[i]))

    weights(0)
    for copy in wz:
        copy.wait_recv()
    weights(1)
    for o in (1, 0):
        partial(o, 0)

    for copy in ins:
        copy.wait()
    mine = pl.ds(pl.multiple_of(worker * PART, 8), PART)
    anchor = fav[mine, :]
    total = anchor - fr[0]
    for j in range(1, WORKERS):
        loc[j - 1].wait_recv()
        total = total + (anchor - fr[j])
    ps[mine, :] = total
    pse = [send(ps.at[mine], ps.at[mine], S_PSE + j - 1, other_worker(j)) for j in range(1, WORKERS)]

    def plane(o):
        for i in range(2):
            for h in range(2):
                r2[o, i, h].wait_recv()
        for h in range(2):
            rows = pl.ds(h * half, half)
            gb[o, gat[o], rows, :] = gb[o, gat[o], rows, :] + load_code(rf.at[o, 0, h]) + load_code(rf.at[o, 1, h])

    plane(1)
    gz = [
        send(code_of(gs.at[h], gb[1, gat[1], pl.ds(h * half, half), :]), zr.at[h], S_GZ + h, partner)
        for h in range(2)
    ]
    forward(0)
    forward(1)
    give(0, gat[0], 0)

    product(1, 0)
    for i in range(2):
        for o in range(2):
            w1[o, 1 - i, i].wait_recv()
            product(o, side[i])
    plane(0)
    for o in range(2):
        for i in range(2):
            w2[o, i].wait_recv()
        product(o, 2)

    for copy in pse:
        copy.wait_recv()
    pseudo = ps[...] / WORKERS
    momentum = outer_mass * omv[...] + pseudo
    nmv[...] = momentum
    nav[...] = fav[...] - outer_rate * (pseudo + outer_mass * momentum)
    results = [local(nmv, nm_ref, L_RES), local(nav, na_ref, L_RES + 1)]

    for h in range(2):
        gz[h].wait_recv()
        rows = pl.ds(h * half, half)
        gradient = gb[0, gat[0], rows, :] + load_code(zr.at[h])
        weight = wv[rows, :]
        first_new = first_decay * fmv[rows, :] + (1.0 - first_decay) * gradient
        second_new = second_decay * smv[rows, :] + (1.0 - second_decay) * gradient * gradient
        first_hat = first_new / (1.0 - first_decay**adam_count)
        second_hat = second_new / (1.0 - second_decay**adam_count)
        nfv[rows, :] = first_new
        nsv[rows, :] = second_new
        nwv[rows, :] = weight - inner_rate * (
            first_hat / (jnp.sqrt(second_hat) + adam_epsilon) + weight_decay * weight
        )
    results += [local(nfv, nf_ref, L_RES + 2), local(nsv, ns_ref, L_RES + 3), local(nwv, nw_ref, L_RES + 4)]

    for copy in out:
        copy.wait_recv()
    for copy in results + out_here:
        copy.wait()
    for copy in sent:
        copy.wait_send()


GROUP = 4


def finish(code_ref, *refs):
    fg_ref = refs[5]
    code, wide, stage, sems = refs[11:]
    groups = code_ref.shape[0] // GROUP
    loads = [
        pltpu.make_async_copy(code_ref.at[pl.ds(i * GROUP, GROUP)], code.at[pl.ds(i * GROUP, GROUP)], sems.at[0, i])
        for i in range(groups)
    ]
    stores = [
        pltpu.make_async_copy(
            wide.at[:, pl.ds(i * GROUP * ROWS, GROUP * ROWS)],
            fg_ref.at[:, pl.ds(i * GROUP * ROWS, GROUP * ROWS)],
            sems.at[1, i],
        )
        for i in range(groups)
    ]
    into = [pltpu.make_async_copy(refs[k], stage.at[k], sems.at[0, groups + k]) for k in range(5)]
    outof = [pltpu.make_async_copy(stage.at[k], refs[6 + k], sems.at[1, groups + k]) for k in range(5)]
    for copy in loads + into:
        copy.start()
    for i in range(groups):
        loads[i].wait()
        for k in range(i * GROUP, (i + 1) * GROUP):
            wide[:, pl.ds(k * ROWS, ROWS)] = load_code(code.at[k])
        stores[i].start()
        if i == groups - 2:
            for load, store in zip(into, outof):
                load.wait()
                store.start()
    for copy in stores + outof:
        copy.wait()


def on_device(
    features, value_cotangent, value_weight, first_moment, second_moment, fragment_local, fragment_anchor,
    outer_momentum,
):
    hbm = pl.BlockSpec(memory_space=pltpu.HBM)
    slabs = features.shape[1] // ROWS
    param = jax.ShapeDtypeStruct((ROWS, COLS), F32)
    vparam = pltpu.VMEM((ROWS, COLS), F32)
    got = pl.pallas_call(
        kernel,
        name="backward",
        out_shape=(jax.ShapeDtypeStruct((slabs, TOK + MARK, ROWS), BF16),) + (param,) * 5,
        in_specs=[hbm] * 8,
        out_specs=(hbm,) * 6,
        scratch_shapes=[
            pltpu.VMEM((2, RING, RING * TOK, ROWS), BF16),
            pltpu.VMEM((2, RING * TOK, COLS), BF16),
            pltpu.VMEM((2, RING, 2, ROWS // 2 + MARK, COLS), BF16),
            pltpu.VMEM((2, RING, ROWS, COLS), F32),
            pltpu.VMEM((2, 2, ROWS // 2 + MARK, COLS), BF16),
            pltpu.VMEM((2, 2, ROWS // 2 + MARK, COLS), BF16),
            pltpu.VMEM((2, 2, 2, ROWS // 2 + MARK, COLS), BF16),
            pltpu.VMEM((2, 2, 2, ROWS // 2 + MARK, COLS), BF16),
            pltpu.VMEM((2, ROWS // 2 + MARK, COLS), BF16),
            pltpu.VMEM((2, ROWS // 2 + MARK, COLS), BF16),
            pltpu.VMEM((2, RING, RING, TOK + MARK, ROWS), BF16),
            pltpu.VMEM((ROWS, COLS), BF16),
            pltpu.VMEM((ROWS, COLS), BF16),
            vparam, vparam, vparam, vparam, vparam,
            pltpu.VMEM((WORKERS, PART, COLS), F32),
            vparam,
            vparam, vparam, vparam, vparam, vparam,
            pltpu.SemaphoreType.DMA((N_REMOTE,)),
            pltpu.SemaphoreType.DMA((N_REMOTE,)),
            pltpu.SemaphoreType.DMA((N_LOCAL,)),
        ],
        compiler_params=pltpu.CompilerParams(
            collective_id=0, has_side_effects=True, vmem_limit_bytes=56 * 2**20
        ),
    )(
        features, value_cotangent, value_weight[0], first_moment[0], second_moment[0], fragment_local[0],
        fragment_anchor, outer_momentum,
    )
    feature_grad, weight_new, first_new, second_new, new_anchor, new_momentum = pl.pallas_call(
        finish,
        name="finish",
        out_shape=(jax.ShapeDtypeStruct(features.shape, F32),) + (param,) * 5,
        in_specs=[hbm] * 6,
        out_specs=(hbm,) * 6,
        scratch_shapes=[
            pltpu.VMEM((slabs, TOK + MARK, ROWS), BF16),
            pltpu.VMEM(features.shape, F32),
            pltpu.VMEM((5, ROWS, COLS), F32),
            pltpu.SemaphoreType.DMA((2, slabs // GROUP + 5)),
        ],
        compiler_params=pltpu.CompilerParams(vmem_limit_bytes=60 * 2**20),
    )(*got)
    return feature_grad, weight_new[None], first_new[None], second_new[None], new_anchor, new_momentum


def solution(mesh):
    tokens = P(("worker", "fsdp"), None)
    groups = P("worker", "fsdp", None)
    whole = P("fsdp", None)
    return jax.shard_map(
        on_device,
        mesh=mesh,
        in_specs=(tokens, tokens, groups, groups, groups, groups, whole, whole),
        out_specs=(tokens, groups, groups, groups, whole, whole),
        check_vma=False,
    )
```

```python
import jax
import jax.numpy as jnp
from jax import lax
from jax.experimental import pallas as pl
from jax.experimental.pallas import tpu as pltpu
from jax.sharding import PartitionSpec as P

MESH = pl.DeviceIdType.MESH
F32 = jnp.float32
BF16 = jnp.bfloat16

first_decay = 0.9
second_decay = 0.95
inner_rate = 0.001
weight_decay = 0.1
adam_epsilon = 1e-08
adam_count = 10.0
outer_rate = 0.7
outer_mass = 0.9

RING = 4
TOK = 192
ROWS = 256
COLS = 512
WORKERS = 8
PART = ROWS // WORKERS

_count = 0


def _take(n):
    global _count
    base = _count
    _count += n
    return base


S_FEAT = _take(2 * 3 * RING)
S_COT1 = _take(8)
S_COT2 = _take(4)
S_WZ = _take(2)
S_W1 = _take(8)
S_W2 = _take(4)
S_R1 = _take(4)
S_R2 = _take(8)
S_GZ = _take(2)
S_OUT = _take(2 * 3 * RING)
S_LOC = _take(WORKERS - 1)
S_PSE = _take(WORKERS - 1)
N_REMOTE = _count

L_FEAT = 0
L_COT = 8
L_W = 10
L_IN = 11
L_OUT = 17
L_RES = 25
N_LOCAL = 30

STEPS = 30847.0
MARK = 8


def encode(t):
    largest = jnp.max(jnp.abs(t), axis=0, keepdims=True)
    unit = jnp.maximum(largest * 1.01, 1e-30).astype(BF16).astype(F32)
    q = t * (STEPS / unit)
    n = jnp.minimum(jnp.floor(jnp.abs(q) + 0.5), STEPS)
    e = jnp.floor(n * (1.0 / 128.0))
    size = (1.0 + (n - 128.0 * e) * (1.0 / 128.0)) * jnp.exp2(e - 120.0)
    return jnp.where(q < 0, -size, size).astype(BF16), unit


def store_code(ref, t):
    code, unit = encode(t)
    rows = t.shape[0]
    ref[pl.ds(0, rows), :] = code
    ref[pl.ds(rows, MARK), :] = jnp.broadcast_to(unit, (MARK, t.shape[1])).astype(BF16)


def code_of(ref, t):
    store_code(ref, t)
    return ref


def load_code(ref):
    rows = ref.shape[0] - MARK
    unit = ref[pl.ds(rows, MARK), :].astype(F32)[0:1]
    return decode(ref[pl.ds(0, rows), :], unit)


def decode(code, unit):
    v = code.astype(F32)
    a = jnp.abs(v)
    e = jnp.floor(jnp.log(a) * 1.4426950408889634 + 0.0025)
    n = a * jnp.exp2(7.0 - e) + (e * 128.0 + 119.0 * 128.0)
    step = unit * (1.0 / STEPS)
    return n * jnp.where(v < 0, -step, step)


def kernel(
    f_ref, c_ref, w_ref, fm_ref, sm_ref, fl_ref, fa_ref, om_ref,
    code_ref, nw_ref, nf_ref, ns_ref, na_ref, nm_ref,
    fb, cb, wb, gb, r1s, rh, r2s, rf, gs, zr, ob, high, low, wv, fmv, smv, fav, omv, fr, ps,
    nwv, nfv, nsv, nav, nmv,
    ssem, rsem, lsem,
):
    worker = lax.axis_index("worker")
    place = lax.axis_index("fsdp")
    x, y, zh = place // 8, (place // 2) % RING, place % 2

    zo = (zh, 1 - zh)
    gat = tuple(x * (1 - z) + y * z for z in zo)
    exc = tuple(y * (1 - z) + x * z for z in zo)

    def along_gather(o, d):
        z = zo[o]
        xx, yy = (x + d * (1 - z)) % RING, (y + d * z) % RING
        return (worker, (xx * RING + yy) * 2 + zh)

    def along_exchange(o, d):
        z = zo[o]
        xx, yy = (x + d * z) % RING, (y + d * (1 - z)) % RING
        return (worker, (xx * RING + yy) * 2 + zh)

    partner = (worker, place + 1 - 2 * zh)

    def other_worker(j):
        return ((worker + j) % WORKERS, place)

    def column(o, g, e):
        z = zo[o]
        start = g * (2048 - 1536 * z) + e * (512 + 1536 * z) + z * ROWS
        return pl.ds(pl.multiple_of(start, ROWS), ROWS)

    def slab(o, g, e):
        z = zo[o]
        return g * (8 - 6 * z) + e * (2 + 6 * z) + z

    def tokens(e, half=None):
        if half is None:
            return pl.ds(pl.multiple_of(e * TOK, 16), TOK)
        return pl.ds(pl.multiple_of(e * TOK + half * (TOK // 2), 16), TOK // 2)

    sent = []

    def send(src, dst, sem, device):
        copy = pltpu.make_async_remote_copy(
            src_ref=src, dst_ref=dst, send_sem=ssem.at[sem], recv_sem=rsem.at[sem],
            device_id=device, device_id_type=MESH,
        )
        copy.start()
        sent.append(copy)
        return copy

    def local(src, dst, sem):
        copy = pltpu.make_async_copy(src, dst, lsem.at[sem])
        copy.start()
        return copy

    barrier = pltpu.get_barrier_semaphore()
    peers = [along_gather(0, d) for d in (1, 2, 3)] + [along_exchange(0, d) for d in (1, 2, 3)]
    peers += [partner] + [other_worker(j) for j in range(1, WORKERS)]
    for peer in peers:
        pl.semaphore_signal(barrier, inc=1, device_id=peer, device_id_type=MESH)

    w_here = local(w_ref, wv, L_W)
    cot_here = [local(c_ref, cb.at[o, tokens(exc[o])], L_COT + o) for o in range(2)]
    feat_here = [
        local(f_ref.at[:, column(o, g, exc[o])], fb.at[o, g, tokens(exc[o])], L_FEAT + o * RING + g)
        for o in range(2)
        for g in range(RING)
    ]
    ins = [
        local(src, dst, L_IN + i)
        for i, (src, dst) in enumerate(
            ((fm_ref, fmv), (sm_ref, smv), (fa_ref, fav), (om_ref, omv),
             (fl_ref.at[pl.ds(pl.multiple_of(worker * PART, 8), PART)], fr.at[0]))
        )
    ]
    half = ROWS // 2
    w_here.wait()
    for h in range(2):
        store_code(wb.at[0, gat[0], h], wv[pl.ds(h * half, half), :])
    pl.semaphore_wait(barrier, len(peers))

    side = (1, RING - 1)

    def halves(i):
        return (i, 1 - i)

    cot1 = {}
    for part in range(2):
        for o in range(2):
            for i in range(2):
                h = halves(i)[part]
                cot1[o, i, h] = send(
                    c_ref.at[pl.ds(h * (TOK // 2), TOK // 2)], cb.at[o, tokens(exc[o], h)],
                    S_COT1 + 4 * o + 2 * i + h, along_exchange(o, side[i]),
                )
    wz = [send(wb.at[0, gat[0], h], wb.at[1, gat[0], h], S_WZ + h, partner) for h in range(2)]
    feat = {}

    def features(at):
        for d in (2, 1, 3):
            for o in range(2):
                feat[o, at, d] = send(
                    f_ref.at[:, column(o, (gat[o] + at) % RING, (exc[o] + d) % RING)],
                    fb.at[o, (gat[o] + at) % RING, tokens(exc[o])],
                    S_FEAT + (o * 3 + d - 1) * RING + at,
                    along_exchange(o, d),
                )

    features(2)

    for copy in cot_here:
        copy.wait()
    cot2 = []
    for o in range(2):
        for i in range(2):
            cot1[o, i, i].wait_recv()
            rows = cb.at[o, tokens((exc[o] + RING - side[i]) % RING, i)]
            cot2.append(send(rows, rows, S_COT2 + 2 * o + i, along_exchange(o, side[i])))
    for at in (1, 3, 0):
        features(at)
    loc = [
        send(
            fl_ref.at[pl.ds(pl.multiple_of((worker + j) % WORKERS * PART, 8), PART)],
            fr.at[j], S_LOC + j - 1, other_worker(j),
        )
        for j in range(1, WORKERS)
    ]

    def multiply(o, g):
        for h in range(2):
            w = load_code(wb.at[o, g, h])
            top = w.astype(BF16)
            high[pl.ds(h * half, half), :] = top
            low[pl.ds(h * half, half), :] = (w - top.astype(F32)).astype(BF16)
        dims = (((1,), (1,)), ((), ()))

        def step(e, carry):
            c = cb[o, tokens(e)]
            t = lax.dot_general(c, high[...], dims, preferred_element_type=F32) + lax.dot_general(
                c, low[...], dims, preferred_element_type=F32
            )
            store_code(ob.at[o, g, e], t)
            return carry

        lax.fori_loop(0, RING, step, 0)

    out = []
    out_here = []

    def give(o, g, at):
        there = code_ref.at[slab(o, g, exc[o])]
        for d in (2, 1, 3):
            out.append(
                send(
                    ob.at[o, g, (exc[o] + d) % RING], there,
                    S_OUT + (o * 3 + d - 1) * RING + at, along_exchange(o, d),
                )
            )
        out_here.append(local(ob.at[o, g, exc[o]], there, L_OUT + o * RING + at))

    def product(o, at):
        g = (gat[o] + at) % RING
        multiply(o, g)
        give(o, g, at)

    for copy in feat_here:
        copy.wait()
    for key in cot1:
        if key[1] != key[2]:
            cot1[key].wait_recv()
    for copy in cot2:
        copy.wait_recv()
    multiply(0, gat[0])

    def partial(o, at):
        g = (gat[o] + at) % RING
        for d in (2, 1, 3):
            feat[o, at, d].wait_recv()
        gb[o, g] = lax.dot_general(
            fb[o, g], cb[o], (((0,), (0,)), ((), ())), preferred_element_type=F32
        )

    r1, r2 = {}, {}
    for o in range(2):
        far = (gat[o] + 2) % RING
        partial(o, 2)
        for i in range(2):
            r1[o, i] = send(
                code_of(r1s.at[o, i], gb[o, far, pl.ds(i * half, half), :]), rh.at[o, i],
                S_R1 + 2 * o + i, along_gather(o, side[i]),
            )

    def hand(o, i, h):
        block = (gat[o] + side[i]) % RING
        r2[o, i, h] = send(
            code_of(r2s.at[o, i, h], gb[o, block, pl.ds(h * half, half), :]), rf.at[o, i, h],
            S_R2 + 4 * o + 2 * i + h, along_gather(o, side[i]),
        )

    for i in range(2):
        for o in range(2):
            partial(o, side[i])
            hand(o, i, 1 - i)
    for o in range(2):
        for i in range(2):
            r1[o, i].wait_recv()
            block = (gat[o] + side[i]) % RING
            rows = pl.ds(i * half, half)
            gb[o, block, rows, :] = gb[o, block, rows, :] + load_code(rh.at[o, i])
            hand(o, i, i)

    w1, w2 = {}, {}

    def weights(o):
        for part in range(2):
            for i in range(2):
                h = halves(i)[part]
                rows = wb.at[o, gat[o], h]
                w1[o, i, h] = send(rows, rows, S_W1 + 4 * o + 2 * i + h, along_gather(o, side[i]))

    def forward(o):
        for i in range(2):
            w1[o, i, i].wait_recv()
            rows = wb.at[o, (gat[o] + RING - side[i]) % RING, i]
            w2[o, i] = send(rows, rows, S_W2 + 2 * o + i, along_gather(o, side[i]))

    weights(0)
    for copy in wz:
        copy.wait_recv()
    weights(1)
    for o in (1, 0):
        partial(o, 0)

    for copy in ins:
        copy.wait()
    mine = pl.ds(pl.multiple_of(worker * PART, 8), PART)
    anchor = fav[mine, :]
    total = anchor - fr[0]
    for j in range(1, WORKERS):
        loc[j - 1].wait_recv()
        total = total + (anchor - fr[j])
    ps[mine, :] = total
    pse = [send(ps.at[mine], ps.at[mine], S_PSE + j - 1, other_worker(j)) for j in range(1, WORKERS)]

    def plane(o):
        for i in range(2):
            for h in range(2):
                r2[o, i, h].wait_recv()
        for h in range(2):
            rows = pl.ds(h * half, half)
            gb[o, gat[o], rows, :] = gb[o, gat[o], rows, :] + load_code(rf.at[o, 0, h]) + load_code(rf.at[o, 1, h])

    plane(1)
    gz = [
        send(code_of(gs.at[h], gb[1, gat[1], pl.ds(h * half, half), :]), zr.at[h], S_GZ + h, partner)
        for h in range(2)
    ]
    forward(0)
    forward(1)
    give(0, gat[0], 0)

    product(1, 0)
    for i in range(2):
        for o in range(2):
            w1[o, 1 - i, i].wait_recv()
            product(o, side[i])
    plane(0)
    for o in range(2):
        for i in range(2):
            w2[o, i].wait_recv()
        product(o, 2)

    for copy in pse:
        copy.wait_recv()
    pseudo = ps[...] / WORKERS
    momentum = outer_mass * omv[...] + pseudo
    nmv[...] = momentum
    nav[...] = fav[...] - outer_rate * (pseudo + outer_mass * momentum)
    results = [local(nmv, nm_ref, L_RES), local(nav, na_ref, L_RES + 1)]

    for h in range(2):
        gz[h].wait_recv()
        rows = pl.ds(h * half, half)
        gradient = gb[0, gat[0], rows, :] + load_code(zr.at[h])
        weight = wv[rows, :]
        first_new = first_decay * fmv[rows, :] + (1.0 - first_decay) * gradient
        second_new = second_decay * smv[rows, :] + (1.0 - second_decay) * gradient * gradient
        first_hat = first_new / (1.0 - first_decay**adam_count)
        second_hat = second_new / (1.0 - second_decay**adam_count)
        nfv[rows, :] = first_new
        nsv[rows, :] = second_new
        nwv[rows, :] = weight - inner_rate * (
            first_hat / (jnp.sqrt(second_hat) + adam_epsilon) + weight_decay * weight
        )
    results += [local(nfv, nf_ref, L_RES + 2), local(nsv, ns_ref, L_RES + 3), local(nwv, nw_ref, L_RES + 4)]

    for copy in out:
        copy.wait_recv()
    for copy in results + out_here:
        copy.wait()
    for copy in sent:
        copy.wait_send()


GROUP = 4


def finish(code_ref, *refs):
    fg_ref = refs[5]
    code, wide, stage, sems = refs[11:]
    groups = code_ref.shape[0] // GROUP
    loads = [
        pltpu.make_async_copy(code_ref.at[pl.ds(i * GROUP, GROUP)], code.at[pl.ds(i * GROUP, GROUP)], sems.at[0, i])
        for i in range(groups)
    ]
    stores = [
        pltpu.make_async_copy(
            wide.at[:, pl.ds(i * GROUP * ROWS, GROUP * ROWS)],
            fg_ref.at[:, pl.ds(i * GROUP * ROWS, GROUP * ROWS)],
            sems.at[1, i],
        )
        for i in range(groups)
    ]
    into = [pltpu.make_async_copy(refs[k], stage.at[k], sems.at[0, groups + k]) for k in range(5)]
    outof = [pltpu.make_async_copy(stage.at[k], refs[6 + k], sems.at[1, groups + k]) for k in range(5)]
    for copy in loads + into:
        copy.start()
    for i in range(groups):
        loads[i].wait()
        for k in range(i * GROUP, (i + 1) * GROUP):
            wide[:, pl.ds(k * ROWS, ROWS)] = load_code(code.at[k])
        stores[i].start()
        if i == groups - 1:
            for load, store in zip(into, outof):
                load.wait()
                store.start()
    for copy in stores + outof:
        copy.wait()


def on_device(
    features, value_cotangent, value_weight, first_moment, second_moment, fragment_local, fragment_anchor,
    outer_momentum,
):
    hbm = pl.BlockSpec(memory_space=pltpu.HBM)
    slabs = features.shape[1] // ROWS
    param = jax.ShapeDtypeStruct((ROWS, COLS), F32)
    vparam = pltpu.VMEM((ROWS, COLS), F32)
    got = pl.pallas_call(
        kernel,
        name="backward",
        out_shape=(jax.ShapeDtypeStruct((slabs, TOK + MARK, ROWS), BF16),) + (param,) * 5,
        in_specs=[hbm] * 8,
        out_specs=(hbm,) * 6,
        scratch_shapes=[
            pltpu.VMEM((2, RING, RING * TOK, ROWS), BF16),
            pltpu.VMEM((2, RING * TOK, COLS), BF16),
            pltpu.VMEM((2, RING, 2, ROWS // 2 + MARK, COLS), BF16),
            pltpu.VMEM((2, RING, ROWS, COLS), F32),
            pltpu.VMEM((2, 2, ROWS // 2 + MARK, COLS), BF16),
            pltpu.VMEM((2, 2, ROWS // 2 + MARK, COLS), BF16),
            pltpu.VMEM((2, 2, 2, ROWS // 2 + MARK, COLS), BF16),
            pltpu.VMEM((2, 2, 2, ROWS // 2 + MARK, COLS), BF16),
            pltpu.VMEM((2, ROWS // 2 + MARK, COLS), BF16),
            pltpu.VMEM((2, ROWS // 2 + MARK, COLS), BF16),
            pltpu.VMEM((2, RING, RING, TOK + MARK, ROWS), BF16),
            pltpu.VMEM((ROWS, COLS), BF16),
            pltpu.VMEM((ROWS, COLS), BF16),
            vparam, vparam, vparam, vparam, vparam,
            pltpu.VMEM((WORKERS, PART, COLS), F32),
            vparam,
            vparam, vparam, vparam, vparam, vparam,
            pltpu.SemaphoreType.DMA((N_REMOTE,)),
            pltpu.SemaphoreType.DMA((N_REMOTE,)),
            pltpu.SemaphoreType.DMA((N_LOCAL,)),
        ],
        compiler_params=pltpu.CompilerParams(
            collective_id=0, has_side_effects=True, vmem_limit_bytes=56 * 2**20
        ),
    )(
        features, value_cotangent, value_weight[0], first_moment[0], second_moment[0], fragment_local[0],
        fragment_anchor, outer_momentum,
    )
    feature_grad, weight_new, first_new, second_new, new_anchor, new_momentum = pl.pallas_call(
        finish,
        name="finish",
        out_shape=(jax.ShapeDtypeStruct(features.shape, F32),) + (param,) * 5,
        in_specs=[hbm] * 6,
        out_specs=(hbm,) * 6,
        scratch_shapes=[
            pltpu.VMEM((slabs, TOK + MARK, ROWS), BF16),
            pltpu.VMEM(features.shape, F32),
            pltpu.VMEM((5, ROWS, COLS), F32),
            pltpu.SemaphoreType.DMA((2, slabs // GROUP + 5)),
        ],
        compiler_params=pltpu.CompilerParams(vmem_limit_bytes=60 * 2**20),
    )(*got)
    return feature_grad, weight_new[None], first_new[None], second_new[None], new_anchor, new_momentum


def solution(mesh):
    tokens = P(("worker", "fsdp"), None)
    groups = P("worker", "fsdp", None)
    whole = P("fsdp", None)
    return jax.shard_map(
        on_device,
        mesh=mesh,
        in_specs=(tokens, tokens, groups, groups, groups, groups, whole, whole),
        out_specs=(tokens, groups, groups, groups, whole, whole),
        check_vma=False,
    )
```
